32 devices in a mesh: runs: 2 (over y), gz: 4 (over x, core), gx: 4 (over z).
Axes of the slice: x: 2, y: 2, z: 4, core: 2. Of those that a mesh axis runs over, the one named last changes fastest.
Arguments:
- magnetic: float32 [3, 64, 64, 1024], P(None, 'gx', 'gz', 'runs'), parts along dimension 3, may hold values from -12 to 12
- friction: float32 [64], P('gz'), may hold values from 0.3 to 3
Outputs:
- relaxed: float32 [3, 64, 64, 1024], P(None, 'gx', 'gz', 'runs'), parts along dimension 3
- potential: float32 [3, 64, 64, 1024], P(None, 'gx', 'gz', 'runs'), parts along dimension 3
The draws below stay inside these ranges and needn't reach their ends.
There are 2 independent parts, one for each index of `runs`. The reference program is written for one: setup_inputs(seed, part) draws one part's arguments, and reference() takes and returns one part's arrays. A program takes and returns all parts, laid end to end along the dimension named above; an argument that names none is the same for every part. Nothing has to cross between parts.
All inputs are finite; a program needn't handle non-finite values.
Results may differ from the reference program's by a relative error of at most 0.00017.
Values sent between devices are 32-bit elements; how exact they have to be, the bound alone decides.
A program may use at most 64 MiB of HBM per device.

```python
import math
import jax
import jax.numpy as jnp

NY = 512
DESCENTS = 2
RELAX = 2
NX = 64
NZ = 64


def draw_magnetic(key, part):
    x_frac = jnp.arange(NX, dtype=jnp.float32) / (NX - 1)
    z_frac = jnp.arange(NZ, dtype=jnp.float32) / (NZ - 1)
    amplitude = 1.7 * jnp.exp(jnp.log(3.0) * (0.5 * x_frac[:, None, None] - z_frac[None, :, None]))
    base = jax.random.truncated_normal(key, -4.0, 4.0, (3, NX, NZ, NY), jnp.float32)
    return (base * amplitude[None]).astype(jnp.float32)


def steps_of(key, extent, pieces, low, high):
    def one(position, shards_of):
        draws = jax.random.uniform(jax.random.fold_in(jax.random.fold_in(key, 6), position), (shards_of,), jnp.float32, low / len(pieces), high / len(pieces))
        return jnp.repeat(jnp.exp(draws), extent[position] // shards_of).reshape((-1,) + (1,) * (len(extent) - position - 1))

    level = one(*pieces[0])
    for cut in pieces[1:]:
        level = level * one(*cut)
    return level


def setup_inputs(seed: int = 0, part: int = 0) -> dict:
    arg_keys = jax.random.split(jax.random.key(seed), 3)
    own_keys = jax.random.split(jax.random.fold_in(arg_keys[2], part), 3)
    magnetic = draw_magnetic(jax.random.fold_in(jax.random.fold_in(arg_keys[2], part), 71), part)
    friction = jnp.clip(jnp.exp(math.log(3.0) - 2.3025851 * jax.random.uniform(arg_keys[1], (NZ,), jnp.float32) ** steps_of(arg_keys[1], (NZ,), ((0, 4),), -0.2, 0.2)), 0.3, 3.0)
    return dict(magnetic=magnetic, friction=friction)


step_scale = 0.5
time_step = 0.2


def diff_x(padded):
    return 0.5 * (padded[..., 2:, 1:-1, :] - padded[..., :-2, 1:-1, :])


def diff_z(padded):
    return 0.5 * (padded[..., 1:-1, 2:, :] - padded[..., 1:-1, :-2, :])


def diff_y(padded):
    middle = padded[..., 1:-1, 1:-1, :]
    return 0.5 * (jnp.roll(middle, -1, axis=-1) - jnp.roll(middle, 1, axis=-1))


def interior(padded):
    return padded[..., 1:-1, 1:-1, :]


def curl_of(padded):
    return jnp.stack([diff_y(padded[2]) - diff_z(padded[1]), diff_z(padded[0]) - diff_x(padded[2]), diff_x(padded[1]) - diff_y(padded[0])])


def divergence(padded):
    return diff_x(padded[0]) + diff_y(padded[1]) + diff_z(padded[2])


def gradient(scalar):
    return jnp.stack([diff_x(scalar), diff_y(scalar), diff_z(scalar)])


def cross_product(left, right):
    return jnp.stack([left[1] * right[2] - left[2] * right[1], left[2] * right[0] - left[0] * right[2], left[0] * right[1] - left[1] * right[0]])


def dot_product(left, right):
    return left[0] * right[0] + left[1] * right[1] + left[2] * right[2]


def pad_rim(values, width):
    return jnp.pad(values, ((0, 0), (width, width), (width, width), (0, 0)))


def omega_parts(widened):
    current = curl_of(widened)
    spread = divergence(widened)
    middle = interior(widened)
    square = jnp.maximum(dot_product(middle, middle), 1.0)
    lorentz = cross_product(current, middle)
    omega_field = (lorentz - spread[None] * middle) / square[None]
    return omega_field, current, spread, lorentz, square


def descent_force(omega_rim, field_rim, omega_core, current, spread, field_core):
    twisted = curl_of(cross_product(omega_rim, field_rim))
    twisted = twisted - cross_product(omega_core, current)
    twisted = twisted - gradient(dot_product(omega_rim, field_rim))
    twisted = twisted + omega_core * spread[None]
    return twisted + dot_product(omega_core, omega_core)[None] * field_core


def reference(magnetic, friction):
    field_now = magnetic
    cell_count = NX * NZ * NY
    for sweep_step in range(DESCENTS):
        widened = pad_rim(field_now, 2)
        omega_rim, current_rim, spread_rim, lorentz_rim, square_rim = omega_parts(widened)
        field_rim = interior(widened)
        omega_core = interior(omega_rim)
        current = interior(current_rim)
        spread = interior(spread_rim)
        lorentz = interior(lorentz_rim)
        square = interior(square_rim)
        descent = descent_force(omega_rim, field_rim, omega_core, current, spread, field_now)
        density = dot_product(lorentz, lorentz) / square + spread * spread
        step_rate = step_scale * (jnp.sum(density) / cell_count) / (jnp.sum(dot_product(descent, descent)) / cell_count + 1e-6)
        field_now = field_now + step_rate * descent
    relaxed = field_now
    columns = jnp.stack([-relaxed[1], relaxed[0]])
    suffix = jnp.flip(jnp.cumsum(jnp.flip(columns, 2), axis=2), 2)
    potential = jnp.concatenate([suffix, jnp.zeros_like(suffix[:1])], 0)
    for sweep_step in range(RELAX):
        induced = curl_of(pad_rim(potential, 1))
        current = curl_of(pad_rim(induced, 1))
        square = jnp.maximum(dot_product(induced, induced), 1.0)
        velocity = cross_product(current, induced) / (friction[None, :, None] * square)[None]
        potential = potential + time_step * cross_product(velocity, induced)
    return relaxed, potential
```

```python
import functools

import jax
import jax.numpy as jnp
from jax import lax
from jax.experimental import pallas as pl
from jax.experimental.pallas import tpu as pltpu
from jax.sharding import PartitionSpec as P

DESCENTS = 2
RELAX = 2
ROUNDS = 1 + (DESCENTS - 1) + RELAX
LANES = 128

step_scale = 0.5
time_step = 0.2

DIRS = ((-1, 0), (1, 0), (0, -1), (0, 1), (-1, -1), (-1, 1), (1, -1), (1, 1))
OPP = (1, 0, 3, 2, 7, 6, 5, 4)


def cross(l, r):
    return [l[1] * r[2] - l[2] * r[1], l[2] * r[0] - l[0] * r[2], l[0] * r[1] - l[1] * r[0]]


def dot(l, r):
    return l[0] * r[0] + l[1] * r[1] + l[2] * r[2]


def kernel(
    gxn, gzn, cx, cz, nb, mag, fric, out_r, out_p,
    fld, pot, fb, eb, xr, zs, zr, cs, cr, ps, pr, ts, tr, above,
    ssem, rsem, psend, precv, tsend, trecv, insem, osem,
):
    gx = lax.axis_index("gx")
    gz = lax.axis_index("gz")
    n = gxn * gzn
    me = gz * gxn + gx
    core = pl.ds(8, cz)
    rim = cz + 8
    f32 = jnp.float32

    def lanes(b):
        return pl.ds(b * LANES, LANES)

    def in_copy(b):
        return pltpu.make_async_copy(
            mag.at[:, :, :, lanes(b)], fld.at[:, pl.ds(2, cx), b, core, :], insem.at[b]
        )

    for b in range(nb):
        in_copy(b).start()

    barrier = pltpu.get_barrier_semaphore()

    def peer(j):
        other = (me + j) % n
        return {"gz": other // gxn, "gx": other % gxn}

    def greet(j, _):
        pl.semaphore_signal(barrier, inc=1, device_id=peer(j), device_id_type=pl.DeviceIdType.MESH)
        return 0

    lax.fori_loop(1, n, greet, 0)

    for ref in (fld, pot):
        for c in range(3):
            for i in (0, 1, cx + 2, cx + 3):
                ref[c, i] = jnp.zeros(ref.shape[2:], f32)

        def clear(i, _):
            for c in range(3):
                for b in range(nb):
                    ref[c, i, b, 0:8, :] = jnp.zeros((8, LANES), f32)
                    ref[c, i, b, cz + 8 : cz + 16, :] = jnp.zeros((8, LANES), f32)
            return 0

        lax.fori_loop(2, cx + 2, clear, 0)

    pl.semaphore_wait(barrier, n - 1)
    for b in range(nb):
        in_copy(b).wait()

    def exists(d):
        dx, dz = DIRS[d]
        tests = []
        if dx:
            tests.append(gx > 0 if dx < 0 else gx < gxn - 1)
        if dz:
            tests.append(gz > 0 if dz < 0 else gz < gzn - 1)
        return functools.reduce(jnp.logical_and, tests)

    def link(r, d, src):
        dx, dz = DIRS[d]
        o = OPP[d]
        if d < 2:
            start = 2 if d == 0 else cx
            s, t = src.at[:, pl.ds(start, 2), :, core, :], xr.at[r, o]
        elif d < 4:
            s, t = zs.at[r, d - 2], zr.at[r, o - 2]
        else:
            s, t = cs.at[r, d - 4], cr.at[r, o - 4]
        return pltpu.make_async_remote_copy(
            src_ref=s, dst_ref=t, send_sem=ssem.at[r, d], recv_sem=rsem.at[r, o],
            device_id={"gz": gz + dz, "gx": gx + dx}, device_id_type=pl.DeviceIdType.MESH,
        )

    def arrival(r, d, src):
        dx, dz = DIRS[d]
        if d < 2:
            s, t = src.at[:, pl.ds(2, 2), :, core, :], xr.at[r, d]
        elif d < 4:
            s, t = zs.at[r, d - 2], zr.at[r, d - 2]
        else:
            s, t = cs.at[r, d - 4], cr.at[r, d - 4]
        return pltpu.make_async_remote_copy(
            src_ref=s, dst_ref=t, send_sem=ssem.at[r, d], recv_sem=rsem.at[r, d],
            device_id={"gz": gz + dz, "gx": gx + dx}, device_id_type=pl.DeviceIdType.MESH,
        )

    def send_halo(r, src):
        for d in (0, 1):
            @pl.when(exists(d))
            def _(d=d):
                link(r, d, src).start()

        def pack(i, _):
            for c in range(3):
                for b in range(nb):
                    zs[r, 0, c, i, 2 * b : 2 * b + 2, :] = src[c, i + 2, b, 8:10, :]
                    zs[r, 1, c, i, 2 * b : 2 * b + 2, :] = src[c, i + 2, b, cz + 6 : cz + 8, :]
            return 0

        lax.fori_loop(0, cx, pack, 0)
        for d in range(4, 8):
            dx, dz = DIRS[d]
            i = 2 if dx < 0 else cx + 1
            k = 8 if dz < 0 else cz + 7
            for c in range(3):
                for b in range(nb):
                    cs[r, d - 4, c, b : b + 1, :] = src[c, i, b, k : k + 1, :]
        for d in range(2, 8):
            @pl.when(exists(d))
            def _(d=d):
                link(r, d, src).start()

    def take_halo(r, src, dst, mu):
        def put(old, new):
            return new if mu is None else old + mu * new

        for d in (2, 3, 4, 5, 6, 7, 0, 1):
            dx, dz = DIRS[d]

            @pl.when(exists(d))
            def _(d=d, dx=dx, dz=dz):
                arrival(r, d, src).wait_recv()
                if d < 2:
                    base = 0 if d == 0 else cx + 2
                    for c in range(3):
                        for p in range(2):
                            for b in range(nb):
                                dst[c, base + p, b, core, :] = put(dst[c, base + p, b, core, :], xr[r, d, c, p, b])
                elif d < 4:
                    row = 6 if d == 2 else cz + 8

                    def unpack(i, _):
                        for c in range(3):
                            for b in range(nb):
                                dst[c, i + 2, b, row : row + 2, :] = put(
                                    dst[c, i + 2, b, row : row + 2, :], zr[r, d - 2, c, i, 2 * b : 2 * b + 2, :]
                                )
                        return 0

                    lax.fori_loop(0, cx, unpack, 0)
                else:
                    i = 1 if dx < 0 else cx + 2
                    k = 7 if dz < 0 else cz + 8
                    for c in range(3):
                        for b in range(nb):
                            dst[c, i, b, k : k + 1, :] = put(dst[c, i, b, k : k + 1, :], cr[r, d - 4, c, b : b + 1, :])
                link(r, d, src).wait_send()

    def differ(ref, comps, i, r0, rows, lane):
        first, last = lane == 0, lane == LANES - 1
        mid = {c: [ref[c, i, b, pl.ds(r0, rows), :] for b in range(nb)] for c in comps}

        def dy(c, b):
            here = mid[c][b]
            nxt, prv = mid[c][(b + 1) % nb], mid[c][(b - 1) % nb]
            up = pltpu.roll(jnp.where(first, nxt, here), LANES - 1, 1)
            down = pltpu.roll(jnp.where(last, prv, here), 1, 1)
            return up - down

        def dx(c, b):
            return ref[c, i + 1, b, pl.ds(r0, rows), :] - ref[c, i - 1, b, pl.ds(r0, rows), :]

        def dz(c, b):
            return ref[c, i, b, pl.ds(r0 + 1, rows), :] - ref[c, i, b, pl.ds(r0 - 1, rows), :]

        return mid, dx, dy, dz

    def folded(v):
        total = v[0:8]
        for k in range(8, v.shape[0], 8):
            total = total + v[k : k + 8]
        return total

    lane_rim = lax.broadcasted_iota(jnp.int32, (rim, LANES), 1)
    row_rim = lax.broadcasted_iota(jnp.int32, (rim, LANES), 0)
    lane_core = lax.broadcasted_iota(jnp.int32, (cz, LANES), 1)
    row_core = lax.broadcasted_iota(jnp.int32, (cz, LANES), 0)
    rows_in = (row_rim >= 1) & (row_rim <= cz)

    def omega_plane(i, acc):
        mid, dx, dy, dz = differ(fld, (0, 1, 2), i, 7, rim, lane_rim)
        rows = pl.ds(7, rim)
        inner = rows_in & ((i >= 2) & (i < cx + 2))
        for b in range(nb):
            B = [mid[c][b] for c in range(3)]
            J = [
                0.5 * (dy(2, b) - dz(1, b)),
                0.5 * (dz(0, b) - dx(2, b)),
                0.5 * (dx(1, b) - dy(0, b)),
            ]
            D = 0.5 * (dx(0, b) + dy(1, b) + dz(2, b))
            inv = 1.0 / jnp.maximum(dot(B, B), 1.0)
            L = cross(J, B)
            om = [(L[c] - D * B[c]) * inv for c in range(3)]
            E = cross(om, B)
            for c in range(3):
                eb[c, i, b, rows, :] = E[c]
            eb[3, i, b, rows, :] = dot(om, B)
            oj = cross(om, J)
            oo = dot(om, om)
            for c in range(3):
                fb[c, i, b, rows, :] = om[c] * D - oj[c] + oo * B[c]
            acc = acc + folded(jnp.where(inner, dot(L, L) * inv + D * D, 0.0))
        return acc

    def force_plane(i, acc):
        mid, dx, dy, dz = differ(eb, (0, 1, 2, 3), i, 8, cz, lane_core)
        for b in range(nb):
            curl = [
                dy(2, b) - dz(1, b) - dx(3, b),
                dz(0, b) - dx(2, b) - dy(3, b),
                dx(1, b) - dy(0, b) - dz(3, b),
            ]
            F = [fb[c, i, b, core, :] + 0.5 * curl[c] for c in range(3)]
            for c in range(3):
                fb[c, i, b, core, :] = F[c]
            acc = acc + folded(dot(F, F))
        return acc

    def psum_copy(s, slot, j):
        return pltpu.make_async_remote_copy(
            src_ref=ps.at[s], dst_ref=pr.at[s, slot], send_sem=psend.at[s, j], recv_sem=precv.at[s, slot],
            device_id=peer(j), device_id_type=pl.DeviceIdType.MESH,
        )

    def send_sums(s, lsum, gsum):
        ps[s, 0:1, :] = jnp.sum(lsum, axis=0, keepdims=True)
        ps[s, 1:2, :] = jnp.sum(gsum, axis=0, keepdims=True)

        def go(j, _):
            psum_copy(s, me, j).start()
            return 0

        lax.fori_loop(1, n, go, 0)

    def take_sums(s):
        pr[s, me] = ps[s]

        def arrive(j, _):
            psum_copy(s, (me + j) % n, j).wait_recv()
            return 0

        lax.fori_loop(1, n, arrive, 0)
        total = lax.fori_loop(0, n, lambda k, t: t + pr[s, k], jnp.zeros((2, LANES), f32))

        def left(j, _):
            psum_copy(s, me, j).wait_send()
            return 0

        lax.fori_loop(1, n, left, 0)
        sums = jnp.sum(total, axis=1, keepdims=True) / (n * cx * cz * nb * LANES)
        return step_scale * sums[0:1] / (sums[1:2] + 1e-6)

    send_halo(0, fld)
    take_halo(0, fld, fld, None)
    zero = jnp.zeros((8, LANES), f32)
    for s in range(DESCENTS):
        lsum = lax.fori_loop(1, cx + 3, omega_plane, zero)
        gsum = lax.fori_loop(2, cx + 2, force_plane, zero)
        send_sums(s, lsum, gsum)
        if s < DESCENTS - 1:
            send_halo(s + 1, fb)
        mu = take_sums(s)

        def update(i, _):
            for c in range(3):
                for b in range(nb):
                    fld[c, i, b, core, :] = fld[c, i, b, core, :] + mu * fb[c, i, b, core, :]
            return 0

        lax.fori_loop(2, cx + 2, update, 0)
        if s < DESCENTS - 1:
            take_halo(s + 1, fb, fld, mu)

    def out_copy(src, out, b, k):
        return pltpu.make_async_copy(
            src.at[:, pl.ds(2, cx), b, core, :], out.at[:, :, :, lanes(b)], osem.at[k, b]
        )

    for b in range(nb):
        out_copy(fld, out_r, b, 0).start()

    def suffix_plane(i, _):
        for c, other, sign in ((0, 1, -1.0), (1, 0, 1.0)):
            for b in range(nb):
                v = sign * fld[other, i, b, core, :]
                step = 1
                while step < cz:
                    v = v + jnp.where(row_core < cz - step, pltpu.roll(v, cz - step, 0), 0.0)
                    step *= 2
                pot[c, i, b, core, :] = v
                ts[c, i - 2, b : b + 1, :] = v[0:1]
        for b in range(nb):
            pot[2, i, b, core, :] = jnp.zeros((cz, LANES), f32)
        return 0

    lax.fori_loop(2, cx + 2, suffix_plane, 0)

    def column_copy(k, dz):
        return pltpu.make_async_remote_copy(
            src_ref=ts, dst_ref=tr.at[k], send_sem=tsend.at[k], recv_sem=trecv.at[k],
            device_id={"gz": gz + dz, "gx": gx}, device_id_type=pl.DeviceIdType.MESH,
        )

    for k in range(1, gzn):
        @pl.when(gz - k >= 0)
        def _(k=k):
            column_copy(k - 1, -k).start()

    above[...] = jnp.zeros(above.shape, f32)
    for k in range(1, gzn):
        @pl.when(gz + k < gzn)
        def _(k=k):
            column_copy(k - 1, k).wait_recv()
            above[...] = above[...] + tr[k - 1]

    def lift(i, _):
        for c in range(2):
            for b in range(nb):
                pot[c, i, b, core, :] = pot[c, i, b, core, :] + above[c, i - 2, b : b + 1, :]
        return 0

    lax.fori_loop(2, cx + 2, lift, 0)
    for k in range(1, gzn):
        @pl.when(gz - k >= 0)
        def _(k=k):
            column_copy(k - 1, -k).wait_send()

    drag = jnp.zeros((cz, LANES), f32)
    for k in range(cz):
        drag = jnp.where(row_core == k, fric[k], drag)
    z_at = gz * cz + row_rim - 1
    z_in = (z_at >= 0) & (z_at < gzn * cz)

    def induced_plane(i, _):
        mid, dx, dy, dz = differ(pot, (0, 1, 2), i, 7, rim, lane_rim)
        x_at = gx * cx + i - 2
        factor = jnp.where(z_in & ((x_at >= 0) & (x_at < gxn * cx)), 0.5, 0.0)
        rows = pl.ds(7, rim)
        for b in range(nb):
            eb[0, i, b, rows, :] = factor * (dy(2, b) - dz(1, b))
            eb[1, i, b, rows, :] = factor * (dz(0, b) - dx(2, b))
            eb[2, i, b, rows, :] = factor * (dx(1, b) - dy(0, b))
        return 0

    def relax_plane(i, _):
        mid, dx, dy, dz = differ(eb, (0, 1, 2), i, 8, cz, lane_core)
        for b in range(nb):
            B = [mid[c][b] for c in range(3)]
            J = [dy(2, b) - dz(1, b), dz(0, b) - dx(2, b), dx(1, b) - dy(0, b)]
            inv = (0.5 * time_step) / (drag * jnp.maximum(dot(B, B), 1.0))
            v = [u * inv for u in cross(J, B)]
            w = cross(v, B)
            for c in range(3):
                pot[c, i, b, core, :] = pot[c, i, b, core, :] + w[c]
        return 0

    for s in range(RELAX):
        r = DESCENTS + s
        send_halo(r, pot)
        take_halo(r, pot, pot, None)
        lax.fori_loop(1, cx + 3, induced_plane, 0)
        lax.fori_loop(2, cx + 2, relax_plane, 0)

    for b in range(nb):
        out_copy(pot, out_p, b, 1).start()
    for k, (src, out) in enumerate(((fld, out_r), (pot, out_p))):
        for b in range(nb):
            out_copy(src, out, b, k).wait()


def body(magnetic, friction):
    _, cx, cz, ny = magnetic.shape
    gxn, gzn = lax.axis_size("gx"), lax.axis_size("gz")
    nb = ny // LANES
    n = gxn * gzn
    full = (cx + 4, nb, cz + 16, LANES)
    VM = lambda *shape: pltpu.VMEM(shape, jnp.float32)
    DMA = lambda *shape: pltpu.SemaphoreType.DMA(shape)
    shape = jax.ShapeDtypeStruct(magnetic.shape, jnp.float32)
    return pl.pallas_call(
        functools.partial(kernel, gxn, gzn, cx, cz, nb),
        out_shape=(shape, shape),
        in_specs=[pl.BlockSpec(memory_space=pl.ANY), pl.BlockSpec(memory_space=pltpu.SMEM)],
        out_specs=(pl.BlockSpec(memory_space=pl.ANY), pl.BlockSpec(memory_space=pl.ANY)),
        scratch_shapes=[
            VM(3, *full), VM(3, *full), VM(3, *full), VM(4, *full),
            VM(ROUNDS, 2, 3, 2, nb, cz, LANES),
            VM(ROUNDS, 2, 3, cx, 2 * nb, LANES), VM(ROUNDS, 2, 3, cx, 2 * nb, LANES),
            VM(ROUNDS, 4, 3, nb, LANES), VM(ROUNDS, 4, 3, nb, LANES),
            VM(DESCENTS, 2, LANES), VM(DESCENTS, n, 2, LANES),
            VM(2, cx, nb, LANES), VM(gzn, 2, cx, nb, LANES), VM(2, cx, nb, LANES),
            DMA(ROUNDS, 8), DMA(ROUNDS, 8),
            DMA(DESCENTS, n), DMA(DESCENTS, n), DMA(gzn), DMA(gzn), DMA(nb), DMA(2, nb),
        ],
        compiler_params=pltpu.CompilerParams(
            collective_id=0, has_side_effects=True, vmem_limit_bytes=48 * 1024 * 1024
        ),
    )(magnetic, friction)


def solution(mesh):
    return jax.shard_map(
        body,
        mesh=mesh,
        in_specs=(P(None, "gx", "gz", "runs"), P("gz")),
        out_specs=(P(None, "gx", "gz", "runs"), P(None, "gx", "gz", "runs")),
        check_vma=False,
    )
```

```python
import functools

import jax
import jax.numpy as jnp
from jax import lax
from jax.experimental import pallas as pl
from jax.experimental.pallas import tpu as pltpu
from jax.sharding import PartitionSpec as P

DESCENTS = 2
RELAX = 2
ROUNDS = 1 + (DESCENTS - 1) + RELAX
LANES = 128

step_scale = 0.5
time_step = 0.2

DIRS = ((-1, 0), (1, 0), (0, -1), (0, 1), (-1, -1), (-1, 1), (1, -1), (1, 1))
PARTS = ((((0, 3, True),),) * DESCENTS + (((1, 2, True), (0, 1, False)),) + (((1, 3, True), (0, 1, False)),) * (RELAX - 1))
ZCOMPS = (3,) * DESCENTS + (2,) + (3,) * (RELAX - 1)
OPP = (1, 0, 3, 2, 7, 6, 5, 4)


def cross(l, r):
    return [l[1] * r[2] - l[2] * r[1], l[2] * r[0] - l[0] * r[2], l[0] * r[1] - l[1] * r[0]]


def dot(l, r):
    return l[0] * r[0] + l[1] * r[1] + l[2] * r[2]


def kernel(
    gxn, gzn, cx, cz, nb, mag, fric, out_r, out_p,
    fld, pot, fb, fb2, eb, xr, zs, zr, cs, cr, ps, pr, ts, tr, above,
    xsend, xrecv, ssem, rsem, psend, precv, tsend, trecv, insem, osem,
):
    gx = lax.axis_index("gx")
    gz = lax.axis_index("gz")
    n = gxn * gzn
    me = gz * gxn + gx
    core = pl.ds(8, cz)
    rim = cz + 8
    f32 = jnp.float32

    def lanes(b):
        return pl.ds(b * LANES, LANES)

    def in_copy(b):
        return pltpu.make_async_copy(
            mag.at[:, :, :, lanes(b)], fld.at[:, pl.ds(2, cx), b, core, :], insem.at[b]
        )

    for b in range(nb):
        in_copy(b).start()

    barrier = pltpu.get_barrier_semaphore()

    def peer(j):
        other = (me + j) % n
        return {"gz": other // gxn, "gx": other % gxn}

    def greet(j, _):
        pl.semaphore_signal(barrier, inc=1, device_id=peer(j), device_id_type=pl.DeviceIdType.MESH)
        return 0

    lax.fori_loop(1, n, greet, 0)

    for ref in (fld, pot):
        for c in range(3):
            for i in (0, 1, cx + 2, cx + 3):
                ref[c, i] = jnp.zeros(ref.shape[2:], f32)

        def clear(i, _):
            for c in range(3):
                for b in range(nb):
                    ref[c, i, b, 0:8, :] = jnp.zeros((8, LANES), f32)
                    ref[c, i, b, cz + 8 : cz + 16, :] = jnp.zeros((8, LANES), f32)
            return 0

        lax.fori_loop(2, cx + 2, clear, 0)

    pl.semaphore_wait(barrier, n - 1)
    for b in range(nb):
        in_copy(b).wait()

    def exists(d):
        dx, dz = DIRS[d]
        tests = []
        if dx:
            tests.append(gx > 0 if dx < 0 else gx < gxn - 1)
        if dz:
            tests.append(gz > 0 if dz < 0 else gz < gzn - 1)
        return functools.reduce(jnp.logical_and, tests)

    def near(side):
        return 1 if side == 0 else 0

    def x_link(r, d, q, src, arriving):
        c0, c1, both = PARTS[r][q]
        slot = d if arriving else OPP[d]
        start = (2 if d == 0 else cx) + (0 if both else near(OPP[d]))
        first, count = (0, 2) if both else (near(slot), 1)
        return pltpu.make_async_remote_copy(
            src_ref=src.at[pl.ds(c0, c1 - c0), pl.ds(start, count), :, core, :],
            dst_ref=xr.at[r, slot, pl.ds(c0, c1 - c0), pl.ds(first, count)],
            send_sem=xsend.at[r, d, q], recv_sem=xrecv.at[r, slot, q],
            device_id={"gz": gz, "gx": gx + DIRS[d][0]}, device_id_type=pl.DeviceIdType.MESH,
        )

    def link(r, d, arriving):
        dx, dz = DIRS[d]
        o = d if arriving else OPP[d]
        if d < 4:
            comps = pl.ds(0, ZCOMPS[r])
            s, t = zs.at[r, d - 2, comps], zr.at[r, o - 2, comps]
        else:
            s, t = cs.at[r, d - 4], cr.at[r, o - 4]
        return pltpu.make_async_remote_copy(
            src_ref=s, dst_ref=t, send_sem=ssem.at[r, d], recv_sem=rsem.at[r, o],
            device_id={"gz": gz + dz, "gx": gx + dx}, device_id_type=pl.DeviceIdType.MESH,
        )

    def send_x(r, src):
        for d in (0, 1):
            @pl.when(exists(d))
            def _(d=d):
                for q in range(len(PARTS[r])):
                    x_link(r, d, q, src, False).start()

    def pack_plane(r, i, src):
        for c in range(ZCOMPS[r]):
            for b in range(nb):
                zs[r, 0, c, i - 2, 2 * b : 2 * b + 2, :] = src[c, i, b, 8:10, :]
                zs[r, 1, c, i - 2, 2 * b : 2 * b + 2, :] = src[c, i, b, cz + 6 : cz + 8, :]

    def send_corners(r, src):
        for d in range(4, 8):
            dx, dz = DIRS[d]
            i = 2 if dx < 0 else cx + 1
            k = 8 if dz < 0 else cz + 7
            for c in range(3):
                for b in range(nb):
                    cs[r, d - 4, c, b : b + 1, :] = src[c, i, b, k : k + 1, :]
        for d in range(4, 8):
            @pl.when(exists(d))
            def _(d=d):
                link(r, d, False).start()

    def send_z(r):
        for d in (2, 3):
            @pl.when(exists(d))
            def _(d=d):
                link(r, d, False).start()

    def loop(low, high, do, unroll=1):
        def step(i, _):
            do(i)
            return 0

        lax.fori_loop(low, high, step, 0, unroll=unroll)

    def put(old, new, mu):
        return new if mu is None else old + mu * new

    def take_z(r, dst, mu):
        for d in (2, 3):
            @pl.when(exists(d))
            def _(d=d):
                link(r, d, True).wait_recv()
                row = 6 if d == 2 else cz + 8

                def unpack(i):
                    for c in range(ZCOMPS[r]):
                        for b in range(nb):
                            dst[c, i + 2, b, row : row + 2, :] = put(
                                dst[c, i + 2, b, row : row + 2, :], zr[r, d - 2, c, i, 2 * b : 2 * b + 2, :], mu
                            )

                loop(0, cx, unpack, 2)
                link(r, d, False).wait_send()

    def take_x(r, src, dst, mu):
        for d in (4, 5, 6, 7):
            dx, dz = DIRS[d]

            @pl.when(exists(d))
            def _(d=d, dx=dx, dz=dz):
                link(r, d, True).wait_recv()
                i = 1 if dx < 0 else cx + 2
                k = 7 if dz < 0 else cz + 8
                for c in range(3):
                    for b in range(nb):
                        dst[c, i, b, k : k + 1, :] = put(dst[c, i, b, k : k + 1, :], cr[r, d - 4, c, b : b + 1, :], mu)
                link(r, d, False).wait_send()

        for d in (0, 1):
            @pl.when(exists(d))
            def _(d=d):
                base = 0 if d == 0 else cx + 2
                for q, (c0, c1, both) in enumerate(PARTS[r]):
                    x_link(r, d, q, src, True).wait_recv()
                    for c in range(c0, c1):
                        for p in range(2) if both else (near(d),):
                            for b in range(nb):
                                dst[c, base + p, b, core, :] = put(
                                    dst[c, base + p, b, core, :], xr[r, d, c, p, b], mu
                                )

        for d in (0, 1):
            @pl.when(exists(d))
            def _(d=d):
                for q in range(len(PARTS[r])):
                    x_link(r, d, q, src, False).wait_send()

    def over_edges(do, acc, low, width):
        def step(j, acc):
            return do(low + j + jnp.where(j >= width, cx + 3 - 2 * low - 2 * width + 1, 0), acc)

        return lax.fori_loop(0, 2 * width, step, acc)

    def differ(ref, comps, i, r0, rows, lane):
        first, last = lane == 0, lane == LANES - 1
        mid = {c: [ref[c, i, b, pl.ds(r0, rows), :] for b in range(nb)] for c in comps}

        def dy(c, b):
            here = mid[c][b]
            nxt, prv = mid[c][(b + 1) % nb], mid[c][(b - 1) % nb]
            up = pltpu.roll(jnp.where(first, nxt, here), LANES - 1, 1)
            down = pltpu.roll(jnp.where(last, prv, here), 1, 1)
            return up - down

        def dx(c, b):
            return ref[c, i + 1, b, pl.ds(r0, rows), :] - ref[c, i - 1, b, pl.ds(r0, rows), :]

        def dz(c, b):
            return ref[c, i, b, pl.ds(r0 + 1, rows), :] - ref[c, i, b, pl.ds(r0 - 1, rows), :]

        return mid, dx, dy, dz

    def folded(v):
        total = v[0:8]
        for k in range(8, v.shape[0], 8):
            total = total + v[k : k + 8]
        return total

    lane_rim = lax.broadcasted_iota(jnp.int32, (rim, LANES), 1)
    row_rim = lax.broadcasted_iota(jnp.int32, (rim, LANES), 0)
    lane_core = lax.broadcasted_iota(jnp.int32, (cz, LANES), 1)
    row_core = lax.broadcasted_iota(jnp.int32, (cz, LANES), 0)
    rows_in = (row_rim >= 1) & (row_rim <= cz)

    def omega_plane(i, acc):
        mid, dx, dy, dz = differ(fld, (0, 1, 2), i, 7, rim, lane_rim)
        rows = pl.ds(7, rim)
        inner = rows_in & ((i >= 2) & (i < cx + 2))
        for b in range(nb):
            B = [mid[c][b] for c in range(3)]
            J = [
                0.5 * (dy(2, b) - dz(1, b)),
                0.5 * (dz(0, b) - dx(2, b)),
                0.5 * (dx(1, b) - dy(0, b)),
            ]
            D = 0.5 * (dx(0, b) + dy(1, b) + dz(2, b))
            inv = 1.0 / jnp.maximum(dot(B, B), 1.0)
            L = cross(J, B)
            om = [(L[c] - D * B[c]) * inv for c in range(3)]
            E = cross(om, B)
            for c in range(3):
                eb[c, i, b, rows, :] = E[c]
            eb[3, i, b, rows, :] = dot(om, B)
            oj = cross(om, J)
            oo = dot(om, om)
            for c in range(3):
                fb[c, i, b, rows, :] = om[c] * D - oj[c] + oo * B[c]
            acc = acc + folded(jnp.where(inner, dot(L, L) * inv + D * D, 0.0))
        return acc

    def force_plane(i, acc):
        mid, dx, dy, dz = differ(eb, (0, 1, 2, 3), i, 8, cz, lane_core)
        for b in range(nb):
            curl = [
                dy(2, b) - dz(1, b) - dx(3, b),
                dz(0, b) - dx(2, b) - dy(3, b),
                dx(1, b) - dy(0, b) - dz(3, b),
            ]
            F = [fb[c, i, b, core, :] + 0.5 * curl[c] for c in range(3)]
            for c in range(3):
                fb2[c, i, b, core, :] = F[c]
            acc = acc + folded(dot(F, F))
        return acc

    def psum_copy(s, slot, j):
        return pltpu.make_async_remote_copy(
            src_ref=ps.at[s], dst_ref=pr.at[s, slot], send_sem=psend.at[s, j], recv_sem=precv.at[s, slot],
            device_id=peer(j), device_id_type=pl.DeviceIdType.MESH,
        )

    def send_sums(s, lsum, gsum):
        ps[s, 0:1, :] = jnp.sum(lsum, axis=0, keepdims=True)
        ps[s, 1:2, :] = jnp.sum(gsum, axis=0, keepdims=True)

        def go(j, _):
            psum_copy(s, me, j).start()
            return 0

        lax.fori_loop(1, n, go, 0)

    def take_sums(s):
        pr[s, me] = ps[s]

        def arrive(j, _):
            psum_copy(s, (me + j) % n, j).wait_recv()
            return 0

        lax.fori_loop(1, n, arrive, 0)
        total = lax.fori_loop(0, n, lambda k, t: t + pr[s, k], jnp.zeros((2, LANES), f32))

        def left(j, _):
            psum_copy(s, me, j).wait_send()
            return 0

        lax.fori_loop(1, n, left, 0)
        sums = jnp.sum(total, axis=1, keepdims=True) / (n * cx * cz * nb * LANES)
        return step_scale * sums[0:1] / (sums[1:2] + 1e-6)

    def suffix_plane(i, src, dst, slot):
        for c, other, sign in ((0, 1, -1.0), (1, 0, 1.0)):
            for b in range(nb):
                v = sign * src[other, i, b, core, :]
                step = 1
                while step < cz:
                    v = v + jnp.where(row_core < cz - step, pltpu.roll(v, cz - step, 0), 0.0)
                    step *= 2
                dst[c, i, b, core, :] = v
                ts[slot, c, i - 2, b : b + 1, :] = v[0:1]

    def column_copy(slot, k, dz):
        return pltpu.make_async_remote_copy(
            src_ref=ts.at[slot], dst_ref=tr.at[slot, k], send_sem=tsend.at[slot, k], recv_sem=trecv.at[slot, k],
            device_id={"gz": gz + dz, "gx": gx}, device_id_type=pl.DeviceIdType.MESH,
        )

    def send_columns(slot):
        for k in range(1, gzn):
            @pl.when(gz - k >= 0)
            def _(k=k):
                column_copy(slot, k - 1, -k).start()

    send_x(0, fld)
    loop(2, cx + 2, lambda i: pack_plane(0, i, fld), 2)
    send_z(0)
    send_corners(0, fld)
    zero = jnp.zeros((8, LANES), f32)
    mu = None
    for s in range(DESCENTS):
        last = s == DESCENTS - 1
        take_z(s, fld, mu)
        lsum = lax.fori_loop(3, cx + 1, omega_plane, zero)
        take_x(s, fld if s == 0 else fb2, fld, mu)
        lsum = over_edges(omega_plane, lsum, 1, 2)

        def force(i, acc):
            acc = force_plane(i, acc)
            if not last:
                pack_plane(s + 1, i, fb2)
            return acc

        gsum = over_edges(force, zero, 2, 2)
        if not last:
            send_x(s + 1, fb2)
            send_corners(s + 1, fb2)
        gsum = lax.fori_loop(4, cx, force, gsum)
        send_sums(s, lsum, gsum)
        if not last:
            send_z(s + 1)
        else:
            loop(2, cx + 2, lambda i: suffix_plane(i, fb2, eb, 1))
            send_columns(1)
        mu = take_sums(s)

        def update(i):
            for c in range(3):
                for b in range(nb):
                    fld[c, i, b, core, :] = fld[c, i, b, core, :] + mu * fb2[c, i, b, core, :]

        if not last:
            loop(2, cx + 2, update)
        if s == DESCENTS - 2:
            loop(2, cx + 2, lambda i: suffix_plane(i, fld, pot, 0))
            send_columns(0)

    above[...] = jnp.zeros(above.shape, f32)
    for k in range(1, gzn):
        @pl.when(gz + k < gzn)
        def _(k=k):
            column_copy(0, k - 1, k).wait_recv()
            column_copy(1, k - 1, k).wait_recv()

            def gather(i):
                for c in range(2):
                    above[c, i] = above[c, i] + (tr[0, k - 1, c, i] + mu * tr[1, k - 1, c, i])

            loop(0, cx, gather, 2)

    def lift(i, acc):
        for c in range(2):
            for b in range(nb):
                pot[c, i, b, core, :] = (pot[c, i, b, core, :] + mu * eb[c, i, b, core, :]) + above[
                    c, i - 2, b : b + 1, :
                ]
        for b in range(nb):
            pot[2, i, b, core, :] = jnp.zeros((cz, LANES), f32)
        pack_plane(DESCENTS, i, pot)
        return acc

    over_edges(lift, 0, 2, 2)
    send_x(DESCENTS, pot)
    lax.fori_loop(4, cx, lift, 0)
    send_z(DESCENTS)
    send_corners(DESCENTS, pot)
    loop(2, cx + 2, update)

    def out_copy(src, out, b, k):
        return pltpu.make_async_copy(
            src.at[:, pl.ds(2, cx), b, core, :], out.at[:, :, :, lanes(b)], osem.at[k, b]
        )

    for b in range(nb):
        out_copy(fld, out_r, b, 0).start()
    for slot in range(2):
        for k in range(1, gzn):
            @pl.when(gz - k >= 0)
            def _(slot=slot, k=k):
                column_copy(slot, k - 1, -k).wait_send()

    drag = jnp.zeros((cz, LANES), f32)
    for k in range(cz):
        drag = jnp.where(row_core == k, fric[k], drag)
    z_at = gz * cz + row_rim - 1
    z_in = (z_at >= 0) & (z_at < gzn * cz)

    def induced_plane(i, acc):
        mid, dx, dy, dz = differ(pot, (0, 1, 2), i, 7, rim, lane_rim)
        x_at = gx * cx + i - 2
        factor = jnp.where(z_in & ((x_at >= 0) & (x_at < gxn * cx)), 0.5, 0.0)
        rows = pl.ds(7, rim)
        for b in range(nb):
            eb[0, i, b, rows, :] = factor * (dy(2, b) - dz(1, b))
            eb[1, i, b, rows, :] = factor * (dz(0, b) - dx(2, b))
            eb[2, i, b, rows, :] = factor * (dx(1, b) - dy(0, b))
        return acc

    def relax_plane(i):
        mid, dx, dy, dz = differ(eb, (0, 1, 2), i, 8, cz, lane_core)
        for b in range(nb):
            B = [mid[c][b] for c in range(3)]
            J = [dy(2, b) - dz(1, b), dz(0, b) - dx(2, b), dx(1, b) - dy(0, b)]
            inv = (0.5 * time_step) / (drag * jnp.maximum(dot(B, B), 1.0))
            v = [u * inv for u in cross(J, B)]
            w = cross(v, B)
            for c in range(3):
                pot[c, i, b, core, :] = pot[c, i, b, core, :] + w[c]

    for s in range(RELAX):
        r = DESCENTS + s
        last = s == RELAX - 1
        take_z(r, pot, None)
        lax.fori_loop(3, cx + 1, induced_plane, 0)
        take_x(r, pot, pot, None)
        over_edges(induced_plane, 0, 1, 2)

        def relax(i, acc):
            relax_plane(i)
            if not last:
                pack_plane(r + 1, i, pot)
            return acc

        if last:
            lax.fori_loop(2, cx + 2, relax, 0)
        else:
            over_edges(relax, 0, 2, 2)
            send_x(r + 1, pot)
            send_corners(r + 1, pot)
            lax.fori_loop(4, cx, relax, 0)
            send_z(r + 1)

    for b in range(nb):
        out_copy(pot, out_p, b, 1).start()
    for k, (src, out) in enumerate(((fld, out_r), (pot, out_p))):
        for b in range(nb):
            out_copy(src, out, b, k).wait()


def body(magnetic, friction):
    _, cx, cz, ny = magnetic.shape
    gxn, gzn = lax.axis_size("gx"), lax.axis_size("gz")
    nb = ny // LANES
    n = gxn * gzn
    full = (cx + 4, nb, cz + 16, LANES)
    VM = lambda *shape: pltpu.VMEM(shape, jnp.float32)
    DMA = lambda *shape: pltpu.SemaphoreType.DMA(shape)
    shape = jax.ShapeDtypeStruct(magnetic.shape, jnp.float32)
    return pl.pallas_call(
        functools.partial(kernel, gxn, gzn, cx, cz, nb),
        out_shape=(shape, shape),
        in_specs=[pl.BlockSpec(memory_space=pltpu.HBM), pl.BlockSpec(memory_space=pltpu.SMEM)],
        out_specs=(pl.BlockSpec(memory_space=pl.ANY), pl.BlockSpec(memory_space=pl.ANY)),
        scratch_shapes=[
            VM(3, *full), VM(3, *full), VM(3, *full), VM(3, *full), VM(4, *full),
            VM(ROUNDS, 2, 3, 2, nb, cz, LANES),
            VM(ROUNDS, 2, 3, cx, 2 * nb, LANES), VM(ROUNDS, 2, 3, cx, 2 * nb, LANES),
            VM(ROUNDS, 4, 3, nb, LANES), VM(ROUNDS, 4, 3, nb, LANES),
            VM(DESCENTS, 2, LANES), VM(DESCENTS, n, 2, LANES),
            VM(2, 2, cx, nb, LANES), VM(2, gzn, 2, cx, nb, LANES), VM(2, cx, nb, LANES),
            DMA(ROUNDS, 2, 2), DMA(ROUNDS, 2, 2),
            DMA(ROUNDS, 8), DMA(ROUNDS, 8),
            DMA(DESCENTS, n), DMA(DESCENTS, n), DMA(2, gzn), DMA(2, gzn), DMA(nb), DMA(2, nb),
        ],
        compiler_params=pltpu.CompilerParams(
            collective_id=0, has_side_effects=True, vmem_limit_bytes=48 * 1024 * 1024
        ),
    )(magnetic, friction)


def solution(mesh):
    return jax.shard_map(
        body,
        mesh=mesh,
        in_specs=(P(None, "gx", "gz", "runs"), P("gz")),
        out_specs=(P(None, "gx", "gz", "runs"), P(None, "gx", "gz", "runs")),
        check_vma=False,
    )
```

```python
import functools

import jax
import jax.numpy as jnp
from jax import lax
from jax.experimental import pallas as pl
from jax.experimental.pallas import tpu as pltpu
from jax.sharding import PartitionSpec as P

DESCENTS = 2
RELAX = 2
ROUNDS = 1 + (DESCENTS - 1) + RELAX
LANES = 128

step_scale = 0.5
time_step = 0.2

DIRS = ((-1, 0), (1, 0), (0, -1), (0, 1), (-1, -1), (-1, 1), (1, -1), (1, 1))
PARTS = ((((0, 3, True),),) * DESCENTS + (((1, 2, True), (0, 1, False)),) + (((1, 3, True), (0, 1, False)),) * (RELAX - 1))
ZCOMPS = (3,) * DESCENTS + (2,) + (3,) * (RELAX - 1)
OPP = (1, 0, 3, 2, 7, 6, 5, 4)


def cross(l, r):
    return [l[1] * r[2] - l[2] * r[1], l[2] * r[0] - l[0] * r[2], l[0] * r[1] - l[1] * r[0]]


def dot(l, r):
    return l[0] * r[0] + l[1] * r[1] + l[2] * r[2]


def kernel(
    gxn, gzn, cx, cz, nb, mag, fric, out_r, out_p,
    fld, pot, fb, fb2, eb, xr, zs, zr, cs, cr, ps, pr, ts, tr, above,
    xsend, xrecv, ssem, rsem, psend, precv, tsend, trecv, insem, osem,
):
    gx = lax.axis_index("gx")
    gz = lax.axis_index("gz")
    n = gxn * gzn
    me = gz * gxn + gx
    core = pl.ds(8, cz)
    rim = cz + 8
    f32 = jnp.float32

    def lanes(b):
        return pl.ds(b * LANES, LANES)

    def in_copy(b):
        return pltpu.make_async_copy(
            mag.at[:, :, :, lanes(b)], fld.at[:, pl.ds(2, cx), b, core, :], insem.at[b]
        )

    for b in range(nb):
        in_copy(b).start()

    barrier = pltpu.get_barrier_semaphore()

    def peer(j):
        other = (me + j) % n
        return {"gz": other // gxn, "gx": other % gxn}

    def greet(j, _):
        pl.semaphore_signal(barrier, inc=1, device_id=peer(j), device_id_type=pl.DeviceIdType.MESH)
        return 0

    lax.fori_loop(1, n, greet, 0)

    for ref in (fld, pot):
        for c in range(3):
            for i in (0, 1, cx + 2, cx + 3):
                ref[c, i] = jnp.zeros(ref.shape[2:], f32)

        def clear(i, _):
            for c in range(3):
                for b in range(nb):
                    ref[c, i, b, 0:8, :] = jnp.zeros((8, LANES), f32)
                    ref[c, i, b, cz + 8 : cz + 16, :] = jnp.zeros((8, LANES), f32)
            return 0

        lax.fori_loop(2, cx + 2, clear, 0)

    for b in range(nb):
        in_copy(b).wait()

    def exists(d):
        dx, dz = DIRS[d]
        tests = []
        if dx:
            tests.append(gx > 0 if dx < 0 else gx < gxn - 1)
        if dz:
            tests.append(gz > 0 if dz < 0 else gz < gzn - 1)
        return functools.reduce(jnp.logical_and, tests)

    def near(side):
        return 1 if side == 0 else 0

    def x_link(r, d, q, src, arriving):
        c0, c1, both = PARTS[r][q]
        slot = d if arriving else OPP[d]
        start = (2 if d == 0 else cx) + (0 if both else near(OPP[d]))
        first, count = (0, 2) if both else (near(slot), 1)
        return pltpu.make_async_remote_copy(
            src_ref=src.at[pl.ds(c0, c1 - c0), pl.ds(start, count), :, core, :],
            dst_ref=xr.at[r, slot, pl.ds(c0, c1 - c0), pl.ds(first, count)],
            send_sem=xsend.at[r, d, q], recv_sem=xrecv.at[r, slot, q],
            device_id={"gz": gz, "gx": gx + DIRS[d][0]}, device_id_type=pl.DeviceIdType.MESH,
        )

    def link(r, d, arriving):
        dx, dz = DIRS[d]
        o = d if arriving else OPP[d]
        if d < 4:
            comps = pl.ds(0, ZCOMPS[r])
            s, t = zs.at[r, d - 2, comps], zr.at[r, o - 2, comps]
        else:
            s, t = cs.at[r, d - 4], cr.at[r, o - 4]
        return pltpu.make_async_remote_copy(
            src_ref=s, dst_ref=t, send_sem=ssem.at[r, d], recv_sem=rsem.at[r, o],
            device_id={"gz": gz + dz, "gx": gx + dx}, device_id_type=pl.DeviceIdType.MESH,
        )

    def send_x(r, src):
        for d in (0, 1):
            @pl.when(exists(d))
            def _(d=d):
                for q in range(len(PARTS[r])):
                    x_link(r, d, q, src, False).start()

    def pack_plane(r, i, src):
        for c in range(ZCOMPS[r]):
            for b in range(nb):
                zs[r, 0, c, i - 2, 2 * b : 2 * b + 2, :] = src[c, i, b, 8:10, :]
                zs[r, 1, c, i - 2, 2 * b : 2 * b + 2, :] = src[c, i, b, cz + 6 : cz + 8, :]

    def pack_corners(r, src):
        for d in range(4, 8):
            dx, dz = DIRS[d]
            i = 2 if dx < 0 else cx + 1
            k = 8 if dz < 0 else cz + 7
            for c in range(3):
                for b in range(nb):
                    cs[r, d - 4, c, b : b + 1, :] = src[c, i, b, k : k + 1, :]

    def send_corners(r):
        for d in range(4, 8):
            @pl.when(exists(d))
            def _(d=d):
                link(r, d, False).start()

    def send_z(r):
        for d in (2, 3):
            @pl.when(exists(d))
            def _(d=d):
                link(r, d, False).start()

    def loop(low, high, do, unroll=1):
        def step(i, _):
            do(i)
            return 0

        lax.fori_loop(low, high, step, 0, unroll=unroll)

    def put(old, new, mu):
        return new if mu is None else old + mu * new

    def take_z(r, dst, mu):
        for d in (2, 3):
            @pl.when(exists(d))
            def _(d=d):
                link(r, d, True).wait_recv()
                row = 6 if d == 2 else cz + 8

                def unpack(i):
                    for c in range(ZCOMPS[r]):
                        for b in range(nb):
                            dst[c, i + 2, b, row : row + 2, :] = put(
                                dst[c, i + 2, b, row : row + 2, :], zr[r, d - 2, c, i, 2 * b : 2 * b + 2, :], mu
                            )

                loop(0, cx, unpack, 2)
                link(r, d, False).wait_send()

    def take_x(r, src, dst, mu):
        for d in (4, 5, 6, 7):
            dx, dz = DIRS[d]

            @pl.when(exists(d))
            def _(d=d, dx=dx, dz=dz):
                link(r, d, True).wait_recv()
                i = 1 if dx < 0 else cx + 2
                k = 7 if dz < 0 else cz + 8
                for c in range(3):
                    for b in range(nb):
                        dst[c, i, b, k : k + 1, :] = put(dst[c, i, b, k : k + 1, :], cr[r, d - 4, c, b : b + 1, :], mu)
                link(r, d, False).wait_send()

        for d in (0, 1):
            @pl.when(exists(d))
            def _(d=d):
                base = 0 if d == 0 else cx + 2
                for q, (c0, c1, both) in enumerate(PARTS[r]):
                    x_link(r, d, q, src, True).wait_recv()
                    for c in range(c0, c1):
                        for p in range(2) if both else (near(d),):
                            for b in range(nb):
                                dst[c, base + p, b, core, :] = put(
                                    dst[c, base + p, b, core, :], xr[r, d, c, p, b], mu
                                )

        for d in (0, 1):
            @pl.when(exists(d))
            def _(d=d):
                for q in range(len(PARTS[r])):
                    x_link(r, d, q, src, False).wait_send()

    def over_edges(do, acc, low, width):
        def step(j, acc):
            return do(low + j + jnp.where(j >= width, cx + 3 - 2 * low - 2 * width + 1, 0), acc)

        return lax.fori_loop(0, 2 * width, step, acc)

    def differ(ref, comps, i, r0, rows, lane):
        first, last = lane == 0, lane == LANES - 1
        mid = {c: [ref[c, i, b, pl.ds(r0, rows), :] for b in range(nb)] for c in comps}

        def dy(c, b):
            here = mid[c][b]
            nxt, prv = mid[c][(b + 1) % nb], mid[c][(b - 1) % nb]
            up = pltpu.roll(jnp.where(first, nxt, here), LANES - 1, 1)
            down = pltpu.roll(jnp.where(last, prv, here), 1, 1)
            return up - down

        def dx(c, b):
            return ref[c, i + 1, b, pl.ds(r0, rows), :] - ref[c, i - 1, b, pl.ds(r0, rows), :]

        def dz(c, b):
            return ref[c, i, b, pl.ds(r0 + 1, rows), :] - ref[c, i, b, pl.ds(r0 - 1, rows), :]

        return mid, dx, dy, dz

    def folded(v):
        total = v[0:8]
        for k in range(8, v.shape[0], 8):
            total = total + v[k : k + 8]
        return total

    lane_rim = lax.broadcasted_iota(jnp.int32, (rim, LANES), 1)
    row_rim = lax.broadcasted_iota(jnp.int32, (rim, LANES), 0)
    lane_core = lax.broadcasted_iota(jnp.int32, (cz, LANES), 1)
    row_core = lax.broadcasted_iota(jnp.int32, (cz, LANES), 0)
    rows_in = (row_rim >= 1) & (row_rim <= cz)

    def omega_plane(i, acc):
        mid, dx, dy, dz = differ(fld, (0, 1, 2), i, 7, rim, lane_rim)
        rows = pl.ds(7, rim)
        inner = rows_in & ((i >= 2) & (i < cx + 2))
        for b in range(nb):
            B = [mid[c][b] for c in range(3)]
            J = [
                0.5 * (dy(2, b) - dz(1, b)),
                0.5 * (dz(0, b) - dx(2, b)),
                0.5 * (dx(1, b) - dy(0, b)),
            ]
            D = 0.5 * (dx(0, b) + dy(1, b) + dz(2, b))
            inv = 1.0 / jnp.maximum(dot(B, B), 1.0)
            L = cross(J, B)
            om = [(L[c] - D * B[c]) * inv for c in range(3)]
            E = cross(om, B)
            for c in range(3):
                eb[c, i, b, rows, :] = E[c]
            eb[3, i, b, rows, :] = dot(om, B)
            oj = cross(om, J)
            oo = dot(om, om)
            for c in range(3):
                fb[c, i, b, rows, :] = om[c] * D - oj[c] + oo * B[c]
            acc = acc + folded(jnp.where(inner, dot(L, L) * inv + D * D, 0.0))
        return acc

    def force_plane(i, acc):
        mid, dx, dy, dz = differ(eb, (0, 1, 2, 3), i, 8, cz, lane_core)
        for b in range(nb):
            curl = [
                dy(2, b) - dz(1, b) - dx(3, b),
                dz(0, b) - dx(2, b) - dy(3, b),
                dx(1, b) - dy(0, b) - dz(3, b),
            ]
            F = [fb[c, i, b, core, :] + 0.5 * curl[c] for c in range(3)]
            for c in range(3):
                fb2[c, i, b, core, :] = F[c]
            acc = acc + folded(dot(F, F))
        return acc

    def psum_copy(s, slot, j):
        return pltpu.make_async_remote_copy(
            src_ref=ps.at[s], dst_ref=pr.at[s, slot], send_sem=psend.at[s, j], recv_sem=precv.at[s, slot],
            device_id=peer(j), device_id_type=pl.DeviceIdType.MESH,
        )

    def send_sums(s, lsum, gsum):
        ps[s, 0:1, :] = jnp.sum(lsum, axis=0, keepdims=True)
        ps[s, 1:2, :] = jnp.sum(gsum, axis=0, keepdims=True)

        def go(j, _):
            psum_copy(s, me, j).start()
            return 0

        lax.fori_loop(1, n, go, 0)

    def take_sums(s):
        pr[s, me] = ps[s]

        def arrive(j, _):
            psum_copy(s, (me + j) % n, j).wait_recv()
            return 0

        lax.fori_loop(1, n, arrive, 0)
        total = lax.fori_loop(0, n, lambda k, t: t + pr[s, k], jnp.zeros((2, LANES), f32))

        def left(j, _):
            psum_copy(s, me, j).wait_send()
            return 0

        lax.fori_loop(1, n, left, 0)
        sums = jnp.sum(total, axis=1, keepdims=True) / (n * cx * cz * nb * LANES)
        return step_scale * sums[0:1] / (sums[1:2] + 1e-6)

    def suffix_plane(i, src, dst):
        for c, other, sign in ((0, 1, -1.0), (1, 0, 1.0)):
            for b in range(nb):
                v = sign * src[other, i, b, core, :]
                step = 1
                while step < cz:
                    v = v + jnp.where(row_core < cz - step, pltpu.roll(v, cz - step, 0), 0.0)
                    step *= 2
                dst[c, i, b, core, :] = v

    def column_plane(i, src, slot):
        for c in range(2):
            for b in range(nb):
                ts[slot, c, i - 2, b : b + 1, :] = src[c, i, b, 8:9, :]

    def column_copy(slot, k, dz):
        return pltpu.make_async_remote_copy(
            src_ref=ts.at[slot], dst_ref=tr.at[slot, k], send_sem=tsend.at[slot, k], recv_sem=trecv.at[slot, k],
            device_id={"gz": gz + dz, "gx": gx}, device_id_type=pl.DeviceIdType.MESH,
        )

    def send_columns(slot):
        for k in range(1, gzn):
            @pl.when(gz - k >= 0)
            def _(k=k):
                column_copy(slot, k - 1, -k).start()

    loop(2, cx + 2, lambda i: pack_plane(0, i, fld), 2)
    pack_corners(0, fld)
    pl.semaphore_wait(barrier, n - 1)
    send_x(0, fld)
    send_z(0)
    send_corners(0)
    loop(2, cx + 2, lambda i: suffix_plane(i, fld, pot))
    zero = jnp.zeros((8, LANES), f32)
    mu = None
    for s in range(DESCENTS):
        last = s == DESCENTS - 1
        take_z(s, fld, mu)
        lsum = lax.fori_loop(3, cx + 1, omega_plane, zero)
        take_x(s, fld if s == 0 else fb2, fld, mu)
        lsum = over_edges(omega_plane, lsum, 1, 2)

        def force(i, acc):
            acc = force_plane(i, acc)
            if not last:
                pack_plane(s + 1, i, fb2)
            return acc

        gsum = over_edges(force, zero, 2, 2)
        if not last:
            send_x(s + 1, fb2)
            pack_corners(s + 1, fb2)
            send_corners(s + 1)
        gsum = lax.fori_loop(4, cx, force, gsum)
        send_sums(s, lsum, gsum)
        if not last:
            send_z(s + 1)
        loop(2, cx + 2, lambda i: suffix_plane(i, fb2, eb))
        if last:
            loop(2, cx + 2, lambda i: column_plane(i, eb, 1), 2)
            send_columns(1)
        mu = take_sums(s)

        def update(i):
            for c in range(3):
                for b in range(nb):
                    fld[c, i, b, core, :] = fld[c, i, b, core, :] + mu * fb2[c, i, b, core, :]

        def advance(i):
            update(i)
            for c in range(2):
                for b in range(nb):
                    pot[c, i, b, core, :] = pot[c, i, b, core, :] + mu * eb[c, i, b, core, :]
            column_plane(i, pot, 0)

        if not last:
            loop(2, cx + 2, advance)
        if s == DESCENTS - 2:
            send_columns(0)

    above[...] = jnp.zeros(above.shape, f32)
    for k in range(1, gzn):
        @pl.when(gz + k < gzn)
        def _(k=k):
            column_copy(0, k - 1, k).wait_recv()
            column_copy(1, k - 1, k).wait_recv()

            def gather(i):
                for c in range(2):
                    above[c, i] = above[c, i] + (tr[0, k - 1, c, i] + mu * tr[1, k - 1, c, i])

            loop(0, cx, gather, 2)

    def lift(i, acc):
        for c in range(2):
            for b in range(nb):
                pot[c, i, b, core, :] = (pot[c, i, b, core, :] + mu * eb[c, i, b, core, :]) + above[
                    c, i - 2, b : b + 1, :
                ]
        for b in range(nb):
            pot[2, i, b, core, :] = jnp.zeros((cz, LANES), f32)
        pack_plane(DESCENTS, i, pot)
        return acc

    over_edges(lift, 0, 2, 2)
    send_x(DESCENTS, pot)
    lax.fori_loop(4, cx, lift, 0)
    send_z(DESCENTS)
    pack_corners(DESCENTS, pot)
    send_corners(DESCENTS)
    loop(2, cx + 2, update)

    def out_copy(src, out, b, k):
        return pltpu.make_async_copy(
            src.at[:, pl.ds(2, cx), b, core, :], out.at[:, :, :, lanes(b)], osem.at[k, b]
        )

    for b in range(nb):
        out_copy(fld, out_r, b, 0).start()
    for slot in range(2):
        for k in range(1, gzn):
            @pl.when(gz - k >= 0)
            def _(slot=slot, k=k):
                column_copy(slot, k - 1, -k).wait_send()

    drag = jnp.zeros((cz, LANES), f32)
    for k in range(cz):
        drag = jnp.where(row_core == k, fric[k], drag)
    z_at = gz * cz + row_rim - 1
    z_in = (z_at >= 0) & (z_at < gzn * cz)

    def induced_plane(i, acc):
        mid, dx, dy, dz = differ(pot, (0, 1, 2), i, 7, rim, lane_rim)
        x_at = gx * cx + i - 2
        factor = jnp.where(z_in & ((x_at >= 0) & (x_at < gxn * cx)), 0.5, 0.0)
        rows = pl.ds(7, rim)
        for b in range(nb):
            eb[0, i, b, rows, :] = factor * (dy(2, b) - dz(1, b))
            eb[1, i, b, rows, :] = factor * (dz(0, b) - dx(2, b))
            eb[2, i, b, rows, :] = factor * (dx(1, b) - dy(0, b))
        return acc

    def relax_plane(i):
        mid, dx, dy, dz = differ(eb, (0, 1, 2), i, 8, cz, lane_core)
        for b in range(nb):
            B = [mid[c][b] for c in range(3)]
            J = [dy(2, b) - dz(1, b), dz(0, b) - dx(2, b), dx(1, b) - dy(0, b)]
            inv = (0.5 * time_step) / (drag * jnp.maximum(dot(B, B), 1.0))
            v = [u * inv for u in cross(J, B)]
            w = cross(v, B)
            for c in range(3):
                pot[c, i, b, core, :] = pot[c, i, b, core, :] + w[c]

    for s in range(RELAX):
        r = DESCENTS + s
        last = s == RELAX - 1
        take_z(r, pot, None)
        lax.fori_loop(3, cx + 1, induced_plane, 0)
        take_x(r, pot, pot, None)
        over_edges(induced_plane, 0, 1, 2)

        def relax(i, acc):
            relax_plane(i)
            if not last:
                pack_plane(r + 1, i, pot)
            return acc

        if last:
            lax.fori_loop(2, cx + 2, relax, 0)
        else:
            over_edges(relax, 0, 2, 2)
            send_x(r + 1, pot)
            pack_corners(r + 1, pot)
            send_corners(r + 1)
            lax.fori_loop(4, cx, relax, 0)
            send_z(r + 1)

    for b in range(nb):
        out_copy(pot, out_p, b, 1).start()
    for k, (src, out) in enumerate(((fld, out_r), (pot, out_p))):
        for b in range(nb):
            out_copy(src, out, b, k).wait()


def body(magnetic, friction):
    _, cx, cz, ny = magnetic.shape
    gxn, gzn = lax.axis_size("gx"), lax.axis_size("gz")
    nb = ny // LANES
    n = gxn * gzn
    full = (cx + 4, nb, cz + 16, LANES)
    VM = lambda *shape: pltpu.VMEM(shape, jnp.float32)
    DMA = lambda *shape: pltpu.SemaphoreType.DMA(shape)
    shape = jax.ShapeDtypeStruct(magnetic.shape, jnp.float32)
    return pl.pallas_call(
        functools.partial(kernel, gxn, gzn, cx, cz, nb),
        out_shape=(shape, shape),
        in_specs=[pl.BlockSpec(memory_space=pltpu.HBM), pl.BlockSpec(memory_space=pltpu.SMEM)],
        out_specs=(pl.BlockSpec(memory_space=pl.ANY), pl.BlockSpec(memory_space=pl.ANY)),
        scratch_shapes=[
            VM(3, *full), VM(3, *full), VM(3, *full), VM(3, *full), VM(4, *full),
            VM(ROUNDS, 2, 3, 2, nb, cz, LANES),
            VM(ROUNDS, 2, 3, cx, 2 * nb, LANES), VM(ROUNDS, 2, 3, cx, 2 * nb, LANES),
            VM(ROUNDS, 4, 3, nb, LANES), VM(ROUNDS, 4, 3, nb, LANES),
            VM(DESCENTS, 2, LANES), VM(DESCENTS, n, 2, LANES),
            VM(2, 2, cx, nb, LANES), VM(2, gzn, 2, cx, nb, LANES), VM(2, cx, nb, LANES),
            DMA(ROUNDS, 2, 2), DMA(ROUNDS, 2, 2),
            DMA(ROUNDS, 8), DMA(ROUNDS, 8),
            DMA(DESCENTS, n), DMA(DESCENTS, n), DMA(2, gzn), DMA(2, gzn), DMA(nb), DMA(2, nb),
        ],
        compiler_params=pltpu.CompilerParams(
            collective_id=0, has_side_effects=True, vmem_limit_bytes=67043328
        ),
    )(magnetic, friction)


def solution(mesh):
    return jax.shard_map(
        body,
        mesh=mesh,
        in_specs=(P(None, "gx", "gz", "runs"), P("gz")),
        out_specs=(P(None, "gx", "gz", "runs"), P(None, "gx", "gz", "runs")),
        check_vma=False,
    )
```

```python
import functools

import jax
import jax.numpy as jnp
from jax import lax
from jax.experimental import pallas as pl
from jax.experimental.pallas import tpu as pltpu
from jax.sharding import PartitionSpec as P

DESCENTS = 2
RELAX = 2
ROUNDS = 1 + (DESCENTS - 1) + RELAX
LANES = 128

step_scale = 0.5
time_step = 0.2

DIRS = ((-1, 0), (1, 0), (0, -1), (0, 1), (-1, -1), (-1, 1), (1, -1), (1, 1))
PARTS = ((((0, 3, True),),) * DESCENTS + (((1, 2, True), (0, 1, False)),) + (((1, 3, True), (0, 1, False)),) * (RELAX - 1))
ZCOMPS = (3,) * DESCENTS + (2,) + (3,) * (RELAX - 1)
OPP = (1, 0, 3, 2, 7, 6, 5, 4)


def cross(l, r):
    return [l[1] * r[2] - l[2] * r[1], l[2] * r[0] - l[0] * r[2], l[0] * r[1] - l[1] * r[0]]


def dot(l, r):
    return l[0] * r[0] + l[1] * r[1] + l[2] * r[2]


def kernel(
    gxn, gzn, cx, cz, nb, mag, fric, out_r, out_p,
    fld, pot, fb, fb2, eb, xr, zs, zr, cs, cr, ps, pr, ts, tr, above,
    xsend, xrecv, ssem, rsem, psend, precv, tsend, trecv, insem, osem,
):
    gx = lax.axis_index("gx")
    gz = lax.axis_index("gz")
    n = gxn * gzn
    me = gz * gxn + gx
    core = pl.ds(8, cz)
    rim = cz + 8
    f32 = jnp.float32

    def lanes(b):
        return pl.ds(b * LANES, LANES)

    def in_copy(b):
        return pltpu.make_async_copy(
            mag.at[:, :, :, lanes(b)], fld.at[:, pl.ds(2, cx), b, core, :], insem.at[b]
        )

    for b in range(nb):
        in_copy(b).start()

    barrier = pltpu.get_barrier_semaphore()

    def peer(j):
        other = (me + j) % n
        return {"gz": other // gxn, "gx": other % gxn}

    def greet(j, _):
        pl.semaphore_signal(barrier, inc=1, device_id=peer(j), device_id_type=pl.DeviceIdType.MESH)
        return 0

    lax.fori_loop(1, n, greet, 0)

    for ref in (fld, pot):
        for c in range(3):
            for i in (0, 1, cx + 2, cx + 3):
                ref[c, i] = jnp.zeros(ref.shape[2:], f32)

        def clear(i, _):
            for c in range(3):
                for b in range(nb):
                    ref[c, i, b, 0:8, :] = jnp.zeros((8, LANES), f32)
                    ref[c, i, b, cz + 8 : cz + 16, :] = jnp.zeros((8, LANES), f32)
            return 0

        lax.fori_loop(2, cx + 2, clear, 0)

    for b in range(nb):
        in_copy(b).wait()

    def exists(d):
        dx, dz = DIRS[d]
        tests = []
        if dx:
            tests.append(gx > 0 if dx < 0 else gx < gxn - 1)
        if dz:
            tests.append(gz > 0 if dz < 0 else gz < gzn - 1)
        return functools.reduce(jnp.logical_and, tests)

    def near(side):
        return 1 if side == 0 else 0

    def x_link(r, d, q, src, arriving):
        c0, c1, both = PARTS[r][q]
        slot = d if arriving else OPP[d]
        start = (2 if d == 0 else cx) + (0 if both else near(OPP[d]))
        first, count = (0, 2) if both else (near(slot), 1)
        return pltpu.make_async_remote_copy(
            src_ref=src.at[pl.ds(c0, c1 - c0), pl.ds(start, count), :, core, :],
            dst_ref=xr.at[r, slot, pl.ds(c0, c1 - c0), pl.ds(first, count)],
            send_sem=xsend.at[r, d, q], recv_sem=xrecv.at[r, slot, q],
            device_id={"gz": gz, "gx": gx + DIRS[d][0]}, device_id_type=pl.DeviceIdType.MESH,
        )

    def link(r, d, arriving):
        dx, dz = DIRS[d]
        o = d if arriving else OPP[d]
        if d < 4:
            comps = pl.ds(0, ZCOMPS[r])
            s, t = zs.at[r, d - 2, comps], zr.at[r, o - 2, comps]
        else:
            s, t = cs.at[r, d - 4], cr.at[r, o - 4]
        return pltpu.make_async_remote_copy(
            src_ref=s, dst_ref=t, send_sem=ssem.at[r, d], recv_sem=rsem.at[r, o],
            device_id={"gz": gz + dz, "gx": gx + dx}, device_id_type=pl.DeviceIdType.MESH,
        )

    def send_x(r, src):
        for d in (0, 1):
            @pl.when(exists(d))
            def _(d=d):
                for q in range(len(PARTS[r])):
                    x_link(r, d, q, src, False).start()

    def pack_plane(r, i, src):
        for c in range(ZCOMPS[r]):
            for b in range(nb):
                zs[r, 0, c, i - 2, 2 * b : 2 * b + 2, :] = src[c, i, b, 8:10, :]
                zs[r, 1, c, i - 2, 2 * b : 2 * b + 2, :] = src[c, i, b, cz + 6 : cz + 8, :]

    def pack_corners(r, src):
        for d in range(4, 8):
            dx, dz = DIRS[d]
            i = 2 if dx < 0 else cx + 1
            k = 8 if dz < 0 else cz + 7
            for c in range(3):
                for b in range(nb):
                    cs[r, d - 4, c, b : b + 1, :] = src[c, i, b, k : k + 1, :]

    def send_corners(r):
        for d in range(4, 8):
            @pl.when(exists(d))
            def _(d=d):
                link(r, d, False).start()

    def send_z(r):
        for d in (2, 3):
            @pl.when(exists(d))
            def _(d=d):
                link(r, d, False).start()

    def loop(low, high, do, unroll=1):
        def step(i, _):
            do(i)
            return 0

        lax.fori_loop(low, high, step, 0, unroll=unroll)

    def put(old, new, mu):
        return new if mu is None else old + mu * new

    def take_z(r, dst, mu):
        for d in (2, 3):
            @pl.when(exists(d))
            def _(d=d):
                link(r, d, True).wait_recv()
                row = 6 if d == 2 else cz + 8

                def unpack(i):
                    for c in range(ZCOMPS[r]):
                        for b in range(nb):
                            dst[c, i + 2, b, row : row + 2, :] = put(
                                dst[c, i + 2, b, row : row + 2, :], zr[r, d - 2, c, i, 2 * b : 2 * b + 2, :], mu
                            )

                loop(0, cx, unpack, 2)
                link(r, d, False).wait_send()

    def take_x(r, src, dst, mu):
        for d in (4, 5, 6, 7):
            dx, dz = DIRS[d]

            @pl.when(exists(d))
            def _(d=d, dx=dx, dz=dz):
                link(r, d, True).wait_recv()
                i = 1 if dx < 0 else cx + 2
                k = 7 if dz < 0 else cz + 8
                for c in range(3):
                    for b in range(nb):
                        dst[c, i, b, k : k + 1, :] = put(dst[c, i, b, k : k + 1, :], cr[r, d - 4, c, b : b + 1, :], mu)
                link(r, d, False).wait_send()

        for d in (0, 1):
            @pl.when(exists(d))
            def _(d=d):
                base = 0 if d == 0 else cx + 2
                for q, (c0, c1, both) in enumerate(PARTS[r]):
                    x_link(r, d, q, src, True).wait_recv()
                    for c in range(c0, c1):
                        for p in range(2) if both else (near(d),):
                            for b in range(nb):
                                dst[c, base + p, b, core, :] = put(
                                    dst[c, base + p, b, core, :], xr[r, d, c, p, b], mu
                                )

        for d in (0, 1):
            @pl.when(exists(d))
            def _(d=d):
                for q in range(len(PARTS[r])):
                    x_link(r, d, q, src, False).wait_send()

    def over_edges(do, acc, low, width):
        def step(j, acc):
            return do(low + j + jnp.where(j >= width, cx + 3 - 2 * low - 2 * width + 1, 0), acc)

        return lax.fori_loop(0, 2 * width, step, acc)

    def differ(ref, comps, i, r0, rows, lane):
        first, last = lane == 0, lane == LANES - 1
        mid = {c: [ref[c, i, b, pl.ds(r0, rows), :] for b in range(nb)] for c in comps}

        def dy(c, b):
            here = mid[c][b]
            nxt, prv = mid[c][(b + 1) % nb], mid[c][(b - 1) % nb]
            up = pltpu.roll(jnp.where(first, nxt, here), LANES - 1, 1)
            down = pltpu.roll(jnp.where(last, prv, here), 1, 1)
            return up - down

        def dx(c, b):
            return ref[c, i + 1, b, pl.ds(r0, rows), :] - ref[c, i - 1, b, pl.ds(r0, rows), :]

        def dz(c, b):
            return ref[c, i, b, pl.ds(r0 + 1, rows), :] - ref[c, i, b, pl.ds(r0 - 1, rows), :]

        return mid, dx, dy, dz

    def folded(v):
        total = v[0:8]
        for k in range(8, v.shape[0], 8):
            total = total + v[k : k + 8]
        return total

    lane_rim = lax.broadcasted_iota(jnp.int32, (rim, LANES), 1)
    row_rim = lax.broadcasted_iota(jnp.int32, (rim, LANES), 0)
    lane_core = lax.broadcasted_iota(jnp.int32, (cz, LANES), 1)
    row_core = lax.broadcasted_iota(jnp.int32, (cz, LANES), 0)
    rows_in = (row_rim >= 1) & (row_rim <= cz)

    def omega_plane(i, acc):
        mid, dx, dy, dz = differ(fld, (0, 1, 2), i, 7, rim, lane_rim)
        rows = pl.ds(7, rim)
        inner = rows_in & ((i >= 2) & (i < cx + 2))
        for b in range(nb):
            B = [mid[c][b] for c in range(3)]
            J = [
                0.5 * (dy(2, b) - dz(1, b)),
                0.5 * (dz(0, b) - dx(2, b)),
                0.5 * (dx(1, b) - dy(0, b)),
            ]
            D = 0.5 * (dx(0, b) + dy(1, b) + dz(2, b))
            square = dot(B, B)
            inv = 1.0 / jnp.maximum(square, 1.0)
            part = square * inv
            L = cross(J, B)
            Li = [u * inv for u in L]
            E = cross(Li, B)
            for c in range(3):
                eb[c, i, b, rows, :] = E[c]
            eb[3, i, b, rows, :] = D * part
            drive = dot(L, Li)
            dd = D * D
            scale = inv * (drive + (dd * part - dd))
            lj = cross(Li, J)
            for c in range(3):
                fb[c, i, b, rows, :] = scale * B[c] - lj[c]
            acc = acc + folded(jnp.where(inner, drive + dd, 0.0))
        return acc

    def force_plane(i, acc):
        mid, dx, dy, dz = differ(eb, (0, 1, 2, 3), i, 8, cz, lane_core)
        for b in range(nb):
            curl = [
                dy(2, b) - dz(1, b) + dx(3, b),
                dz(0, b) - dx(2, b) + dy(3, b),
                dx(1, b) - dy(0, b) + dz(3, b),
            ]
            F = [fb[c, i, b, core, :] + 0.5 * curl[c] for c in range(3)]
            for c in range(3):
                fb2[c, i, b, core, :] = F[c]
            acc = acc + folded(dot(F, F))
        return acc

    def psum_copy(s, slot, j):
        return pltpu.make_async_remote_copy(
            src_ref=ps.at[s], dst_ref=pr.at[s, slot], send_sem=psend.at[s, j], recv_sem=precv.at[s, slot],
            device_id=peer(j), device_id_type=pl.DeviceIdType.MESH,
        )

    def send_sums(s, lsum, gsum):
        ps[s, 0:1, :] = jnp.sum(lsum, axis=0, keepdims=True)
        ps[s, 1:2, :] = jnp.sum(gsum, axis=0, keepdims=True)

        def go(j, _):
            psum_copy(s, me, j).start()
            return 0

        lax.fori_loop(1, n, go, 0)

    def take_sums(s):
        pr[s, me] = ps[s]

        def arrive(j, _):
            psum_copy(s, (me + j) % n, j).wait_recv()
            return 0

        lax.fori_loop(1, n, arrive, 0)
        total = lax.fori_loop(0, n, lambda k, t: t + pr[s, k], jnp.zeros((2, LANES), f32))

        def left(j, _):
            psum_copy(s, me, j).wait_send()
            return 0

        lax.fori_loop(1, n, left, 0)
        sums = jnp.sum(total, axis=1, keepdims=True) / (n * cx * cz * nb * LANES)
        return step_scale * sums[0:1] / (sums[1:2] + 1e-6)

    def suffix_plane(i, src, dst):
        for c, other, sign in ((0, 1, -1.0), (1, 0, 1.0)):
            for b in range(nb):
                v = sign * src[other, i, b, core, :]
                step = 1
                while step < cz:
                    v = v + jnp.where(row_core < cz - step, pltpu.roll(v, cz - step, 0), 0.0)
                    step *= 2
                dst[c, i, b, core, :] = v

    def column_plane(i, src, slot):
        for c in range(2):
            for b in range(nb):
                ts[slot, c, i - 2, b : b + 1, :] = src[c, i, b, 8:9, :]

    def column_copy(slot, k, dz):
        return pltpu.make_async_remote_copy(
            src_ref=ts.at[slot], dst_ref=tr.at[slot, k], send_sem=tsend.at[slot, k], recv_sem=trecv.at[slot, k],
            device_id={"gz": gz + dz, "gx": gx}, device_id_type=pl.DeviceIdType.MESH,
        )

    def send_columns(slot):
        for k in range(1, gzn):
            @pl.when(gz - k >= 0)
            def _(k=k):
                column_copy(slot, k - 1, -k).start()

    loop(2, cx + 2, lambda i: pack_plane(0, i, fld), 2)
    pack_corners(0, fld)
    pl.semaphore_wait(barrier, n - 1)
    send_x(0, fld)
    send_z(0)
    send_corners(0)
    loop(2, cx + 2, lambda i: suffix_plane(i, fld, pot))
    zero = jnp.zeros((8, LANES), f32)
    mu = None
    for s in range(DESCENTS):
        last = s == DESCENTS - 1
        take_z(s, fld, mu)
        lsum = lax.fori_loop(3, cx + 1, omega_plane, zero)
        take_x(s, fld if s == 0 else fb2, fld, mu)
        lsum = over_edges(omega_plane, lsum, 1, 2)

        def force(i, acc):
            acc = force_plane(i, acc)
            if not last:
                pack_plane(s + 1, i, fb2)
            return acc

        gsum = over_edges(force, zero, 2, 2)
        if not last:
            send_x(s + 1, fb2)
            pack_corners(s + 1, fb2)
            send_corners(s + 1)
        gsum = lax.fori_loop(4, cx, force, gsum)
        send_sums(s, lsum, gsum)
        if not last:
            send_z(s + 1)
        loop(2, cx + 2, lambda i: suffix_plane(i, fb2, eb))
        if last:
            loop(2, cx + 2, lambda i: column_plane(i, eb, 1), 2)
            send_columns(1)
        mu = take_sums(s)

        def update(i):
            for c in range(3):
                for b in range(nb):
                    fld[c, i, b, core, :] = fld[c, i, b, core, :] + mu * fb2[c, i, b, core, :]

        def advance(i):
            update(i)
            for c in range(2):
                for b in range(nb):
                    pot[c, i, b, core, :] = pot[c, i, b, core, :] + mu * eb[c, i, b, core, :]
            column_plane(i, pot, 0)

        if not last:
            loop(2, cx + 2, advance)
        if s == DESCENTS - 2:
            send_columns(0)

    above[...] = jnp.zeros(above.shape, f32)
    for k in range(1, gzn):
        @pl.when(gz + k < gzn)
        def _(k=k):
            column_copy(0, k - 1, k).wait_recv()
            column_copy(1, k - 1, k).wait_recv()

            def gather(i):
                for c in range(2):
                    above[c, i] = above[c, i] + (tr[0, k - 1, c, i] + mu * tr[1, k - 1, c, i])

            loop(0, cx, gather, 2)

    def lift(i, acc):
        for c in range(2):
            for b in range(nb):
                pot[c, i, b, core, :] = (pot[c, i, b, core, :] + mu * eb[c, i, b, core, :]) + above[
                    c, i - 2, b : b + 1, :
                ]
        for b in range(nb):
            pot[2, i, b, core, :] = jnp.zeros((cz, LANES), f32)
        pack_plane(DESCENTS, i, pot)
        return acc

    over_edges(lift, 0, 2, 2)
    send_x(DESCENTS, pot)
    lax.fori_loop(4, cx, lift, 0)
    send_z(DESCENTS)
    pack_corners(DESCENTS, pot)
    send_corners(DESCENTS)
    loop(2, cx + 2, update)

    def out_copy(src, out, b, k):
        return pltpu.make_async_copy(
            src.at[:, pl.ds(2, cx), b, core, :], out.at[:, :, :, lanes(b)], osem.at[k, b]
        )

    for b in range(nb):
        out_copy(fld, out_r, b, 0).start()
    for slot in range(2):
        for k in range(1, gzn):
            @pl.when(gz - k >= 0)
            def _(slot=slot, k=k):
                column_copy(slot, k - 1, -k).wait_send()

    drag = jnp.zeros((cz, LANES), f32)
    for k in range(cz):
        drag = jnp.where(row_core == k, fric[k], drag)
    z_at = gz * cz + row_rim - 1
    z_in = (z_at >= 0) & (z_at < gzn * cz)

    def induced_plane(i, acc):
        mid, dx, dy, dz = differ(pot, (0, 1, 2), i, 7, rim, lane_rim)
        x_at = gx * cx + i - 2
        factor = jnp.where(z_in & ((x_at >= 0) & (x_at < gxn * cx)), 0.5, 0.0)
        rows = pl.ds(7, rim)
        for b in range(nb):
            eb[0, i, b, rows, :] = factor * (dy(2, b) - dz(1, b))
            eb[1, i, b, rows, :] = factor * (dz(0, b) - dx(2, b))
            eb[2, i, b, rows, :] = factor * (dx(1, b) - dy(0, b))
        return acc

    def relax_plane(i):
        mid, dx, dy, dz = differ(eb, (0, 1, 2), i, 8, cz, lane_core)
        for b in range(nb):
            B = [mid[c][b] for c in range(3)]
            J = [dy(2, b) - dz(1, b), dz(0, b) - dx(2, b), dx(1, b) - dy(0, b)]
            inv = (0.5 * time_step) / (drag * jnp.maximum(dot(B, B), 1.0))
            v = [u * inv for u in cross(J, B)]
            w = cross(v, B)
            for c in range(3):
                pot[c, i, b, core, :] = pot[c, i, b, core, :] + w[c]

    for s in range(RELAX):
        r = DESCENTS + s
        last = s == RELAX - 1
        take_z(r, pot, None)
        lax.fori_loop(3, cx + 1, induced_plane, 0)
        take_x(r, pot, pot, None)
        over_edges(induced_plane, 0, 1, 2)

        def relax(i, acc):
            relax_plane(i)
            if not last:
                pack_plane(r + 1, i, pot)
            return acc

        if last:
            lax.fori_loop(2, cx + 2, relax, 0)
        else:
            over_edges(relax, 0, 2, 2)
            send_x(r + 1, pot)
            pack_corners(r + 1, pot)
            send_corners(r + 1)
            lax.fori_loop(4, cx, relax, 0)
            send_z(r + 1)

    for b in range(nb):
        out_copy(pot, out_p, b, 1).start()
    for k, (src, out) in enumerate(((fld, out_r), (pot, out_p))):
        for b in range(nb):
            out_copy(src, out, b, k).wait()


def body(magnetic, friction):
    _, cx, cz, ny = magnetic.shape
    gxn, gzn = lax.axis_size("gx"), lax.axis_size("gz")
    nb = ny // LANES
    n = gxn * gzn
    full = (cx + 4, nb, cz + 16, LANES)
    VM = lambda *shape: pltpu.VMEM(shape, jnp.float32)
    DMA = lambda *shape: pltpu.SemaphoreType.DMA(shape)
    shape = jax.ShapeDtypeStruct(magnetic.shape, jnp.float32)
    return pl.pallas_call(
        functools.partial(kernel, gxn, gzn, cx, cz, nb),
        out_shape=(shape, shape),
        in_specs=[pl.BlockSpec(memory_space=pltpu.HBM), pl.BlockSpec(memory_space=pltpu.SMEM)],
        out_specs=(pl.BlockSpec(memory_space=pl.ANY), pl.BlockSpec(memory_space=pl.ANY)),
        scratch_shapes=[
            VM(3, *full), VM(3, *full), VM(3, *full), VM(3, *full), VM(4, *full),
            VM(ROUNDS, 2, 3, 2, nb, cz, LANES),
            VM(ROUNDS, 2, 3, cx, 2 * nb, LANES), VM(ROUNDS, 2, 3, cx, 2 * nb, LANES),
            VM(ROUNDS, 4, 3, nb, LANES), VM(ROUNDS, 4, 3, nb, LANES),
            VM(DESCENTS, 2, LANES), VM(DESCENTS, n, 2, LANES),
            VM(2, 2, cx, nb, LANES), VM(2, gzn, 2, cx, nb, LANES), VM(2, cx, nb, LANES),
            DMA(ROUNDS, 2, 2), DMA(ROUNDS, 2, 2),
            DMA(ROUNDS, 8), DMA(ROUNDS, 8),
            DMA(DESCENTS, n), DMA(DESCENTS, n), DMA(2, gzn), DMA(2, gzn), DMA(nb), DMA(2, nb),
        ],
        compiler_params=pltpu.CompilerParams(
            collective_id=0, has_side_effects=True, vmem_limit_bytes=48 * 1024 * 1024
        ),
    )(magnetic, friction)


def solution(mesh):
    return jax.shard_map(
        body,
        mesh=mesh,
        in_specs=(P(None, "gx", "gz", "runs"), P("gz")),
        out_specs=(P(None, "gx", "gz", "runs"), P(None, "gx", "gz", "runs")),
        check_vma=False,
    )
```

```python
import functools

import jax
import jax.numpy as jnp
from jax import lax
from jax.experimental import pallas as pl
from jax.experimental.pallas import tpu as pltpu
from jax.sharding import PartitionSpec as P

DESCENTS = 2
RELAX = 2
ROUNDS = 1 + (DESCENTS - 1) + RELAX
LANES = 128

step_scale = 0.5
time_step = 0.2

DIRS = ((-1, 0), (1, 0), (0, -1), (0, 1), (-1, -1), (-1, 1), (1, -1), (1, 1))
PARTS = ((((0, 3, True),),) * DESCENTS + (((1, 2, True), (0, 1, False)),) + (((1, 3, True), (0, 1, False)),) * (RELAX - 1))
ZCOMPS = (3,) * DESCENTS + (2,) + (3,) * (RELAX - 1)
OPP = (1, 0, 3, 2, 7, 6, 5, 4)


def cross(l, r):
    return [l[1] * r[2] - l[2] * r[1], l[2] * r[0] - l[0] * r[2], l[0] * r[1] - l[1] * r[0]]


def dot(l, r):
    return l[0] * r[0] + l[1] * r[1] + l[2] * r[2]


def kernel(
    gxn, gzn, cx, cz, nb, mag, fric, out_r, out_p,
    fld, pot, fb, fb2, eb, xr, zs, zr, cs, cr, ps, pr, ts, tr, above,
    xsend, xrecv, zsend, zrecv, ssem, rsem, psend, precv, tsend, trecv, insem, osem,
):
    gx = lax.axis_index("gx")
    gz = lax.axis_index("gz")
    n = gxn * gzn
    me = gz * gxn + gx
    core = pl.ds(8, cz)
    rim = cz + 8
    f32 = jnp.float32

    def lanes(b):
        return pl.ds(b * LANES, LANES)

    def in_copy(b):
        return pltpu.make_async_copy(
            mag.at[:, :, :, lanes(b)], fld.at[:, pl.ds(2, cx), b, core, :], insem.at[b]
        )

    for b in range(nb):
        in_copy(b).start()

    barrier = pltpu.get_barrier_semaphore()

    def peer(j):
        other = (me + j) % n
        return {"gz": other // gxn, "gx": other % gxn}

    def greet(j, _):
        pl.semaphore_signal(barrier, inc=1, device_id=peer(j), device_id_type=pl.DeviceIdType.MESH)
        return 0

    lax.fori_loop(1, n, greet, 0)

    for ref in (fld, pot):
        for c in range(3):
            for i in (0, 1, cx + 2, cx + 3):
                ref[c, i] = jnp.zeros(ref.shape[2:], f32)

        def clear(i, _):
            for c in range(3):
                for b in range(nb):
                    ref[c, i, b, 0:8, :] = jnp.zeros((8, LANES), f32)
                    ref[c, i, b, cz + 8 : cz + 16, :] = jnp.zeros((8, LANES), f32)
            return 0

        lax.fori_loop(2, cx + 2, clear, 0)

    for b in range(nb):
        in_copy(b).wait()

    def exists(d):
        dx, dz = DIRS[d]
        tests = []
        if dx:
            tests.append(gx > 0 if dx < 0 else gx < gxn - 1)
        if dz:
            tests.append(gz > 0 if dz < 0 else gz < gzn - 1)
        return functools.reduce(jnp.logical_and, tests)

    def near(side):
        return 1 if side == 0 else 0

    def x_link(r, d, q, src, arriving):
        c0, c1, both = PARTS[r][q]
        slot = d if arriving else OPP[d]
        start = (2 if d == 0 else cx) + (0 if both else near(OPP[d]))
        first, count = (0, 2) if both else (near(slot), 1)
        return pltpu.make_async_remote_copy(
            src_ref=src.at[pl.ds(c0, c1 - c0), pl.ds(start, count), :, core, :],
            dst_ref=xr.at[r, slot, pl.ds(c0, c1 - c0), pl.ds(first, count)],
            send_sem=xsend.at[r, d, q], recv_sem=xrecv.at[r, slot, q],
            device_id={"gz": gz, "gx": gx + DIRS[d][0]}, device_id_type=pl.DeviceIdType.MESH,
        )

    half = cx // 2

    def z_link(r, d, h, arriving):
        o = d if arriving else OPP[d]
        comps, planes = pl.ds(0, ZCOMPS[r]), pl.ds(h * half, half)
        return pltpu.make_async_remote_copy(
            src_ref=zs.at[r, d - 2, comps, planes], dst_ref=zr.at[r, o - 2, comps, planes],
            send_sem=zsend.at[r, d - 2, h], recv_sem=zrecv.at[r, o - 2, h],
            device_id={"gz": gz + DIRS[d][1], "gx": gx}, device_id_type=pl.DeviceIdType.MESH,
        )

    def link(r, d, arriving):
        dx, dz = DIRS[d]
        o = d if arriving else OPP[d]
        return pltpu.make_async_remote_copy(
            src_ref=cs.at[r, d - 4], dst_ref=cr.at[r, o - 4], send_sem=ssem.at[r, d], recv_sem=rsem.at[r, o],
            device_id={"gz": gz + dz, "gx": gx + dx}, device_id_type=pl.DeviceIdType.MESH,
        )

    def send_x(r, src):
        for d in (0, 1):
            @pl.when(exists(d))
            def _(d=d):
                for q in range(len(PARTS[r])):
                    x_link(r, d, q, src, False).start()

    def pack_plane(r, i, src):
        for c in range(ZCOMPS[r]):
            for b in range(nb):
                zs[r, 0, c, i - 2, 2 * b : 2 * b + 2, :] = src[c, i, b, 8:10, :]
                zs[r, 1, c, i - 2, 2 * b : 2 * b + 2, :] = src[c, i, b, cz + 6 : cz + 8, :]

    def pack_corners(r, src):
        for d in range(4, 8):
            dx, dz = DIRS[d]
            i = 2 if dx < 0 else cx + 1
            k = 8 if dz < 0 else cz + 7
            for c in range(3):
                for b in range(nb):
                    cs[r, d - 4, c, b : b + 1, :] = src[c, i, b, k : k + 1, :]

    def send_corners(r):
        for d in range(4, 8):
            @pl.when(exists(d))
            def _(d=d):
                link(r, d, False).start()

    def send_z(r, h):
        for d in (2, 3):
            @pl.when(exists(d))
            def _(d=d):
                z_link(r, d, h, False).start()

    def loop(low, high, do, unroll=1):
        def step(i, _):
            do(i)
            return 0

        lax.fori_loop(low, high, step, 0, unroll=unroll)

    def put(old, new, mu):
        return new if mu is None else old + mu * new

    def take_z(r, dst, mu, h):
        for d in (2, 3):
            @pl.when(exists(d))
            def _(d=d):
                z_link(r, d, h, True).wait_recv()
                row = 6 if d == 2 else cz + 8

                def unpack(i):
                    for c in range(ZCOMPS[r]):
                        for b in range(nb):
                            dst[c, i + 2, b, row : row + 2, :] = put(
                                dst[c, i + 2, b, row : row + 2, :], zr[r, d - 2, c, i, 2 * b : 2 * b + 2, :], mu
                            )

                loop(h * half, h * half + half, unpack, 2)
                z_link(r, d, h, False).wait_send()

    def inner_planes(r, dst, mu, do, acc):
        for h in range(2):
            take_z(r, dst, mu, h)
            low, high = (3, half + 1) if h == 0 else (half + 1, cx + 1)
            acc = lax.fori_loop(low, high, do, acc)
        return acc

    def later_planes(r, do, acc):
        acc = lax.fori_loop(4, half + 2, do, acc)
        send_z(r, 0)
        acc = lax.fori_loop(half + 2, cx, do, acc)
        send_z(r, 1)
        return acc

    def take_x(r, src, dst, mu):
        for d in (4, 5, 6, 7):
            dx, dz = DIRS[d]

            @pl.when(exists(d))
            def _(d=d, dx=dx, dz=dz):
                link(r, d, True).wait_recv()
                i = 1 if dx < 0 else cx + 2
                k = 7 if dz < 0 else cz + 8
                for c in range(3):
                    for b in range(nb):
                        dst[c, i, b, k : k + 1, :] = put(dst[c, i, b, k : k + 1, :], cr[r, d - 4, c, b : b + 1, :], mu)
                link(r, d, False).wait_send()

        for d in (0, 1):
            @pl.when(exists(d))
            def _(d=d):
                base = 0 if d == 0 else cx + 2
                for q, (c0, c1, both) in enumerate(PARTS[r]):
                    x_link(r, d, q, src, True).wait_recv()
                    for c in range(c0, c1):
                        for p in range(2) if both else (near(d),):
                            for b in range(nb):
                                dst[c, base + p, b, core, :] = put(
                                    dst[c, base + p, b, core, :], xr[r, d, c, p, b], mu
                                )

        for d in (0, 1):
            @pl.when(exists(d))
            def _(d=d):
                for q in range(len(PARTS[r])):
                    x_link(r, d, q, src, False).wait_send()

    def over_edges(do, acc, low, width):
        def step(j, acc):
            return do(low + j + jnp.where(j >= width, cx + 3 - 2 * low - 2 * width + 1, 0), acc)

        return lax.fori_loop(0, 2 * width, step, acc)

    def differ(ref, comps, i, r0, rows, lane):
        first, last = lane == 0, lane == LANES - 1
        mid = {c: [ref[c, i, b, pl.ds(r0, rows), :] for b in range(nb)] for c in comps}

        def dy(c, b):
            here = mid[c][b]
            nxt, prv = mid[c][(b + 1) % nb], mid[c][(b - 1) % nb]
            up = pltpu.roll(jnp.where(first, nxt, here), LANES - 1, 1)
            down = pltpu.roll(jnp.where(last, prv, here), 1, 1)
            return up - down

        def dx(c, b):
            return ref[c, i + 1, b, pl.ds(r0, rows), :] - ref[c, i - 1, b, pl.ds(r0, rows), :]

        def dz(c, b):
            return ref[c, i, b, pl.ds(r0 + 1, rows), :] - ref[c, i, b, pl.ds(r0 - 1, rows), :]

        return mid, dx, dy, dz

    def folded(v):
        total = v[0:8]
        for k in range(8, v.shape[0], 8):
            total = total + v[k : k + 8]
        return total

    lane_rim = lax.broadcasted_iota(jnp.int32, (rim, LANES), 1)
    row_rim = lax.broadcasted_iota(jnp.int32, (rim, LANES), 0)
    lane_core = lax.broadcasted_iota(jnp.int32, (cz, LANES), 1)
    row_core = lax.broadcasted_iota(jnp.int32, (cz, LANES), 0)
    rows_in = (row_rim >= 1) & (row_rim <= cz)

    def omega_plane(i, acc):
        mid, dx, dy, dz = differ(fld, (0, 1, 2), i, 7, rim, lane_rim)
        rows = pl.ds(7, rim)
        inner = rows_in & ((i >= 2) & (i < cx + 2))
        for b in range(nb):
            B = [mid[c][b] for c in range(3)]
            J = [
                0.5 * (dy(2, b) - dz(1, b)),
                0.5 * (dz(0, b) - dx(2, b)),
                0.5 * (dx(1, b) - dy(0, b)),
            ]
            D = 0.5 * (dx(0, b) + dy(1, b) + dz(2, b))
            square = dot(B, B)
            inv = 1.0 / jnp.maximum(square, 1.0)
            part = square * inv
            L = cross(J, B)
            Li = [u * inv for u in L]
            E = cross(Li, B)
            for c in range(3):
                eb[c, i, b, rows, :] = E[c]
            eb[3, i, b, rows, :] = D * part
            drive = dot(L, Li)
            dd = D * D
            scale = inv * (drive + (dd * part - dd))
            lj = cross(Li, J)
            for c in range(3):
                fb[c, i, b, rows, :] = scale * B[c] - lj[c]
            acc = acc + folded(jnp.where(inner, drive + dd, 0.0))
        return acc

    def force_plane(i, acc):
        mid, dx, dy, dz = differ(eb, (0, 1, 2, 3), i, 8, cz, lane_core)
        for b in range(nb):
            curl = [
                dy(2, b) - dz(1, b) + dx(3, b),
                dz(0, b) - dx(2, b) + dy(3, b),
                dx(1, b) - dy(0, b) + dz(3, b),
            ]
            F = [fb[c, i, b, core, :] + 0.5 * curl[c] for c in range(3)]
            for c in range(3):
                fb2[c, i, b, core, :] = F[c]
            acc = acc + folded(dot(F, F))
        return acc

    def psum_copy(s, slot, j):
        return pltpu.make_async_remote_copy(
            src_ref=ps.at[s], dst_ref=pr.at[s, slot], send_sem=psend.at[s, j], recv_sem=precv.at[s, slot],
            device_id=peer(j), device_id_type=pl.DeviceIdType.MESH,
        )

    def send_sums(s, lsum, gsum):
        ps[s, 0:1, :] = jnp.sum(lsum, axis=0, keepdims=True)
        ps[s, 1:2, :] = jnp.sum(gsum, axis=0, keepdims=True)

        def go(j, _):
            psum_copy(s, me, j).start()
            return 0

        lax.fori_loop(1, n, go, 0)

    def take_sums(s):
        pr[s, me] = ps[s]

        def arrive(j, _):
            psum_copy(s, (me + j) % n, j).wait_recv()
            return 0

        lax.fori_loop(1, n, arrive, 0)
        total = lax.fori_loop(0, n, lambda k, t: t + pr[s, k], jnp.zeros((2, LANES), f32))

        def left(j, _):
            psum_copy(s, me, j).wait_send()
            return 0

        lax.fori_loop(1, n, left, 0)
        sums = jnp.sum(total, axis=1, keepdims=True) / (n * cx * cz * nb * LANES)
        return step_scale * sums[0:1] / (sums[1:2] + 1e-6)

    def suffix_plane(i, src, dst):
        for c, other, sign in ((0, 1, -1.0), (1, 0, 1.0)):
            for b in range(nb):
                v = sign * src[other, i, b, core, :]
                step = 1
                while step < cz:
                    v = v + jnp.where(row_core < cz - step, pltpu.roll(v, cz - step, 0), 0.0)
                    step *= 2
                dst[c, i, b, core, :] = v

    def column_plane(i, src, slot):
        for c in range(2):
            for b in range(nb):
                ts[slot, c, i - 2, b : b + 1, :] = src[c, i, b, 8:9, :]

    def column_copy(slot, k, dz):
        return pltpu.make_async_remote_copy(
            src_ref=ts.at[slot], dst_ref=tr.at[slot, k], send_sem=tsend.at[slot, k], recv_sem=trecv.at[slot, k],
            device_id={"gz": gz + dz, "gx": gx}, device_id_type=pl.DeviceIdType.MESH,
        )

    def send_columns(slot):
        for k in range(1, gzn):
            @pl.when(gz - k >= 0)
            def _(k=k):
                column_copy(slot, k - 1, -k).start()

    loop(2, cx + 2, lambda i: pack_plane(0, i, fld), 2)
    pack_corners(0, fld)
    pl.semaphore_wait(barrier, n - 1)
    send_x(0, fld)
    send_z(0, 0)
    send_z(0, 1)
    send_corners(0)
    loop(2, cx + 2, lambda i: suffix_plane(i, fld, pot))
    zero = jnp.zeros((8, LANES), f32)
    mu = None
    for s in range(DESCENTS):
        last = s == DESCENTS - 1
        lsum = inner_planes(s, fld, mu, omega_plane, zero)
        take_x(s, fld if s == 0 else fb2, fld, mu)
        lsum = over_edges(omega_plane, lsum, 1, 2)

        def force(i, acc):
            acc = force_plane(i, acc)
            if not last:
                pack_plane(s + 1, i, fb2)
            return acc

        gsum = over_edges(force, zero, 2, 2)
        if not last:
            send_x(s + 1, fb2)
            pack_corners(s + 1, fb2)
            send_corners(s + 1)
            gsum = later_planes(s + 1, force, gsum)
        else:
            gsum = lax.fori_loop(4, cx, force, gsum)
        send_sums(s, lsum, gsum)
        loop(2, cx + 2, lambda i: suffix_plane(i, fb2, eb))
        if last:
            loop(2, cx + 2, lambda i: column_plane(i, eb, 1), 2)
            send_columns(1)
        mu = take_sums(s)

        def update(i):
            for c in range(3):
                for b in range(nb):
                    fld[c, i, b, core, :] = fld[c, i, b, core, :] + mu * fb2[c, i, b, core, :]

        def advance(i):
            update(i)
            for c in range(2):
                for b in range(nb):
                    pot[c, i, b, core, :] = pot[c, i, b, core, :] + mu * eb[c, i, b, core, :]
            column_plane(i, pot, 0)

        if not last:
            loop(2, cx + 2, advance)
        if s == DESCENTS - 2:
            send_columns(0)

    above[...] = jnp.zeros(above.shape, f32)
    for k in range(1, gzn):
        @pl.when(gz + k < gzn)
        def _(k=k):
            column_copy(0, k - 1, k).wait_recv()
            column_copy(1, k - 1, k).wait_recv()

            def gather(i):
                for c in range(2):
                    above[c, i] = above[c, i] + (tr[0, k - 1, c, i] + mu * tr[1, k - 1, c, i])

            loop(0, cx, gather, 2)

    def lift(i, acc):
        for c in range(2):
            for b in range(nb):
                pot[c, i, b, core, :] = (pot[c, i, b, core, :] + mu * eb[c, i, b, core, :]) + above[
                    c, i - 2, b : b + 1, :
                ]
        for b in range(nb):
            pot[2, i, b, core, :] = jnp.zeros((cz, LANES), f32)
        pack_plane(DESCENTS, i, pot)
        return acc

    over_edges(lift, 0, 2, 2)
    send_x(DESCENTS, pot)
    later_planes(DESCENTS, lift, 0)
    pack_corners(DESCENTS, pot)
    send_corners(DESCENTS)
    loop(2, cx + 2, update)

    def out_copy(src, out, b, k):
        return pltpu.make_async_copy(
            src.at[:, pl.ds(2, cx), b, core, :], out.at[:, :, :, lanes(b)], osem.at[k, b]
        )

    for b in range(nb):
        out_copy(fld, out_r, b, 0).start()
    for slot in range(2):
        for k in range(1, gzn):
            @pl.when(gz - k >= 0)
            def _(slot=slot, k=k):
                column_copy(slot, k - 1, -k).wait_send()

    drag = jnp.zeros((cz, LANES), f32)
    for k in range(cz):
        drag = jnp.where(row_core == k, fric[k], drag)
    z_at = gz * cz + row_rim - 1
    z_in = (z_at >= 0) & (z_at < gzn * cz)

    def induced_plane(i, acc):
        mid, dx, dy, dz = differ(pot, (0, 1, 2), i, 7, rim, lane_rim)
        x_at = gx * cx + i - 2
        factor = jnp.where(z_in & ((x_at >= 0) & (x_at < gxn * cx)), 0.5, 0.0)
        rows = pl.ds(7, rim)
        for b in range(nb):
            eb[0, i, b, rows, :] = factor * (dy(2, b) - dz(1, b))
            eb[1, i, b, rows, :] = factor * (dz(0, b) - dx(2, b))
            eb[2, i, b, rows, :] = factor * (dx(1, b) - dy(0, b))
        return acc

    def relax_plane(i):
        mid, dx, dy, dz = differ(eb, (0, 1, 2), i, 8, cz, lane_core)
        for b in range(nb):
            B = [mid[c][b] for c in range(3)]
            J = [dy(2, b) - dz(1, b), dz(0, b) - dx(2, b), dx(1, b) - dy(0, b)]
            inv = (0.5 * time_step) / (drag * jnp.maximum(dot(B, B), 1.0))
            v = [u * inv for u in cross(J, B)]
            w = cross(v, B)
            for c in range(3):
                pot[c, i, b, core, :] = pot[c, i, b, core, :] + w[c]

    for s in range(RELAX):
        r = DESCENTS + s
        last = s == RELAX - 1
        inner_planes(r, pot, None, induced_plane, 0)
        take_x(r, pot, pot, None)
        over_edges(induced_plane, 0, 1, 2)

        def relax(i, acc):
            relax_plane(i)
            if not last:
                pack_plane(r + 1, i, pot)
            return acc

        if last:
            lax.fori_loop(2, cx + 2, relax, 0)
        else:
            over_edges(relax, 0, 2, 2)
            send_x(r + 1, pot)
            pack_corners(r + 1, pot)
            send_corners(r + 1)
            later_planes(r + 1, relax, 0)

    for b in range(nb):
        out_copy(pot, out_p, b, 1).start()
    for k, (src, out) in enumerate(((fld, out_r), (pot, out_p))):
        for b in range(nb):
            out_copy(src, out, b, k).wait()


def body(magnetic, friction):
    _, cx, cz, ny = magnetic.shape
    gxn, gzn = lax.axis_size("gx"), lax.axis_size("gz")
    nb = ny // LANES
    n = gxn * gzn
    full = (cx + 4, nb, cz + 16, LANES)
    VM = lambda *shape: pltpu.VMEM(shape, jnp.float32)
    DMA = lambda *shape: pltpu.SemaphoreType.DMA(shape)
    shape = jax.ShapeDtypeStruct(magnetic.shape, jnp.float32)
    return pl.pallas_call(
        functools.partial(kernel, gxn, gzn, cx, cz, nb),
        out_shape=(shape, shape),
        in_specs=[pl.BlockSpec(memory_space=pltpu.HBM), pl.BlockSpec(memory_space=pltpu.SMEM)],
        out_specs=(pl.BlockSpec(memory_space=pl.ANY), pl.BlockSpec(memory_space=pl.ANY)),
        scratch_shapes=[
            VM(3, *full), VM(3, *full), VM(3, *full), VM(3, *full), VM(4, *full),
            VM(ROUNDS, 2, 3, 2, nb, cz, LANES),
            VM(ROUNDS, 2, 3, cx, 2 * nb, LANES), VM(ROUNDS, 2, 3, cx, 2 * nb, LANES),
            VM(ROUNDS, 4, 3, nb, LANES), VM(ROUNDS, 4, 3, nb, LANES),
            VM(DESCENTS, 2, LANES), VM(DESCENTS, n, 2, LANES),
            VM(2, 2, cx, nb, LANES), VM(2, gzn, 2, cx, nb, LANES), VM(2, cx, nb, LANES),
            DMA(ROUNDS, 2, 2), DMA(ROUNDS, 2, 2), DMA(ROUNDS, 2, 2), DMA(ROUNDS, 2, 2),
            DMA(ROUNDS, 8), DMA(ROUNDS, 8),
            DMA(DESCENTS, n), DMA(DESCENTS, n), DMA(2, gzn), DMA(2, gzn), DMA(nb), DMA(2, nb),
        ],
        compiler_params=pltpu.CompilerParams(
            collective_id=0, has_side_effects=True, vmem_limit_bytes=48 * 1024 * 1024
        ),
    )(magnetic, friction)


def solution(mesh):
    return jax.shard_map(
        body,
        mesh=mesh,
        in_specs=(P(None, "gx", "gz", "runs"), P("gz")),
        out_specs=(P(None, "gx", "gz", "runs"), P(None, "gx", "gz", "runs")),
        check_vma=False,
    )
```
